128 devices in a mesh: gx: 16 (over z, y), gy: 8 (over x, core).
Axes of the slice: x: 4, y: 4, z: 4, core: 2. Of those that a mesh axis runs over, the one named last changes fastest.
Arguments:
- disp_now: float32 [3, 8, 256, 1024], P(None, None, 'gx', 'gy'), may hold values from -6 to 6
- disp_prev: float32 [3, 8, 256, 1024], P(None, None, 'gx', 'gy'), may hold values from -6 to 6
- density: float32 [8, 256, 1024], P(None, 'gx', 'gy'), may hold values from 1 to 2
- moduli: float32 [2, 8, 256, 1024], P(None, None, 'gx', 'gy'), may hold values from 0.3 to 1
- coarse: float32 [256, 24, 256], P(('gx', 'gy')), may hold values from -6 to 6
- block_route: int32 [256], replicated, may hold values from 0 to 511, as said below
- ranges: int32 [16, 8, 2], P('gx', 'gy'), may hold values from 1 to 8, as said below
- offsets: int32 [16, 8, 4, 3], P('gx', 'gy'), may hold values from 0 to 24, as said below
Outputs:
- incident: float32 [2, 3, 8, 256, 1024], P(None, None, None, 'gx', 'gy')
- disp_mid: float32 [3, 8, 256, 1024], P(None, None, 'gx', 'gy')
- disp_next: float32 [3, 8, 256, 1024], P(None, None, 'gx', 'gy')
The draws below stay inside these ranges and needn't reach their ends.
Inputs may be any that keep to these rules, and one draw needn't show every extreme that they name: block_route[b] = tile 4 + g with tile = X 8 + Y; no slot is named twice; the slots named of a tile are g = 0 to k - 1 for its count k, which is 1 on half of the tiles, 2 on a quarter and 4 on a quarter. ranges[X, Y] = (lo, hi) with hi = 2 k for the tile's count k in block_route, and 1 <= lo < hi. offsets[X, Y, g] = (oz, oe, on) in fine cells with oz at most 5.
All inputs are finite; a program needn't handle non-finite values.
Results may differ from the reference program's by a relative error of at most 0.000073.
Values sent between devices are 32-bit elements; how exact they have to be, the bound alone decides.
A program may use at most 64 MiB of HBM per device.

```python
import math
import jax
import jax.numpy as jnp
from jax import lax

LEV = 8
CE = 16
CN = 128
NT = 4
G = 4
CEC = 8
CNC = 26
PTS = 256
TILES = 128
BLOCKS = 256
NE = 256
NN = 1024
N_GX = 16
N_GY = 8


def plan_tiles(key):
    tile_perm = jax.random.permutation(jax.random.fold_in(key, 101), TILES)
    tile_rank = jnp.argsort(tile_perm).astype(jnp.int32)
    quarter = TILES // 4
    counts = jnp.where(tile_rank < quarter, G, jnp.where(tile_rank < 2 * quarter, 2, 1)).astype(jnp.int32)
    slot_ids = jnp.arange(TILES * G, dtype=jnp.int32)
    slot_tile = slot_ids // G
    slot_group = slot_ids % G
    unused = (slot_group >= counts[slot_tile]).astype(jnp.int32)
    slot_key = unused * (TILES * G) + tile_rank[slot_tile] * G + slot_group
    ordered = jnp.argsort(slot_key)[:BLOCKS].astype(jnp.int32)
    spread_perm = jax.random.permutation(jax.random.fold_in(key, 102), BLOCKS).astype(jnp.int32)
    position = jnp.arange(BLOCKS, dtype=jnp.int32)
    place_key = 4 + spread_perm
    place_key = jnp.where(position == 0, 0, place_key)
    place_key = jnp.where(position == 1, 1, place_key)
    place_key = jnp.where(position == 2 * N_GY, 2, place_key)
    place_key = jnp.where(position == 2 * N_GY + 1, 3, place_key)
    place_rank = jnp.argsort(jnp.argsort(place_key)).astype(jnp.int32)
    routing = ordered[place_rank]
    high_level = 2 * counts
    low_level = jax.random.randint(jax.random.fold_in(key, 103), (TILES,), 1, high_level)
    ranges = jnp.stack([low_level, high_level], axis=-1).reshape(N_GX, N_GY, 2)
    return (routing.astype(jnp.int32), ranges.astype(jnp.int32))


def draw_block_route(key, part):
    return plan_tiles(key)[0]


def draw_ranges(key, part):
    return plan_tiles(key)[1]


def draw_offsets(key, part):
    level_part = jax.random.randint(jax.random.fold_in(key, 201), (N_GX, N_GY, G, 1), 0, 6)
    east_part = jax.random.randint(jax.random.fold_in(key, 202), (N_GX, N_GY, G, 1), 0, 25)
    north_part = jax.random.randint(jax.random.fold_in(key, 203), (N_GX, N_GY, G, 1), 0, 25)
    return jnp.concatenate([level_part, east_part, north_part], axis=-1).astype(jnp.int32)


def block_levels(own_key, shape, shards, least, largest):
    loudness = 1.0
    for dim, shards_of in shards:
        draws = jax.random.uniform(jax.random.fold_in(jax.random.fold_in(own_key, 6), dim), (shards_of,), jnp.float32, least / len(shards), largest / len(shards))
        loudness = loudness * jnp.repeat(jnp.exp(draws), shape[dim] // shards_of).reshape((-1,) + (1,) * (len(shape) - 1 - dim))
    return loudness


def normal_values(own_key, extent, scale, limit, split=(), kind=jnp.bfloat16):
    drawn = jax.random.normal(own_key, extent, jnp.float32) * scale
    if len(split) > 0:
        drawn = block_levels(own_key, extent, split, -0.22, 0.18) * drawn
    return jnp.clip(drawn, min=-limit, max=limit).astype(kind)


def setup_inputs(seed: int = 0) -> dict:
    splits = jax.random.split(jax.random.key(seed), 9)
    return {
        "disp_now": normal_values(splits[0], (3, LEV, NE, NN), 1.0, 6.0, ((2, 16), (3, 8)), jnp.float32),
        "disp_prev": normal_values(splits[1], (3, LEV, NE, NN), 1.0, 6.0, ((2, 16), (3, 8)), jnp.float32),
        "density": jnp.clip(jnp.exp(math.log(2.0) - 0.6931472 * jax.random.uniform(splits[2], (LEV, NE, NN), jnp.float32) ** block_levels(splits[2], (LEV, NE, NN), ((1, 16), (2, 8)), -0.2, 0.2)), 1.0, 2.0),
        "moduli": jnp.clip(jnp.exp(math.log(1.0) - 1.2039728 * jax.random.uniform(splits[3], (2, LEV, NE, NN), jnp.float32) ** block_levels(splits[3], (2, LEV, NE, NN), ((2, 16), (3, 8)), -0.2, 0.2)), 0.3, 1.0),
        "coarse": normal_values(splits[4], (BLOCKS, NT * 6, PTS), 1.0, 6.0, ((0, 128),), jnp.float32),
        "block_route": draw_block_route(jax.random.fold_in(splits[8], 71), 0),
        "ranges": draw_ranges(jax.random.fold_in(splits[8], 71), 0),
        "offsets": draw_offsets(jax.random.fold_in(splits[8], 71), 0),
    }


step_square = 0.05
time_weights = ((-0.0595, 0.7735, 0.3315, -0.0455), (-0.063756, 0.607068, 0.517132, -0.060444))


def trimmed(values_in, axis_pos, head_cut, tail_cut):
    axis_pos = axis_pos % values_in.ndim
    return lax.slice_in_dim(values_in, head_cut, values_in.shape[axis_pos] - tail_cut, axis=axis_pos)


def inner_cut(values_in, axes_list):
    for axis_pos in axes_list:
        values_in = trimmed(values_in, axis_pos, 1, 1)
    return values_in


def operate(motion, shear_mod, lame_mod):
    spatial = (-3, -2, -1)
    stiffness = lame_mod + 2.0 * shear_mod
    components = []
    for i in range(3):
        component = motion[..., i, :, :, :]
        total = None
        for j in range(3):
            axis_along = spatial[j]
            others = tuple(a for a in spatial if a != axis_along)
            modulus = stiffness if j == i else shear_mod
            values = inner_cut(component, others)
            weights = inner_cut(modulus, others)
            middle = trimmed(values, axis_along, 1, 1)
            forward = trimmed(values, axis_along, 2, 0)
            backward = trimmed(values, axis_along, 0, 2)
            modulus_mid = trimmed(weights, axis_along, 1, 1)
            modulus_next = trimmed(weights, axis_along, 2, 0)
            modulus_prior = trimmed(weights, axis_along, 0, 2)
            flux_term = 0.5 * (modulus_mid + modulus_next) * (forward - middle) - 0.5 * (modulus_mid + modulus_prior) * (middle - backward)
            total = flux_term if total is None else total + flux_term
        for j in range(3):
            if j != i:
                across = spatial[i]
                axis_along = spatial[j]
                third_axis = [a for a in spatial if a != across and a != axis_along][0]
                partner = motion[..., j, :, :, :]
                gradient = 0.5 * (trimmed(partner, axis_along, 2, 0) - trimmed(partner, axis_along, 0, 2))
                flux_term = trimmed(lame_mod, axis_along, 1, 1) * gradient
                total = total + trimmed(0.5 * (trimmed(flux_term, across, 2, 0) - trimmed(flux_term, across, 0, 2)), third_axis, 1, 1)
                gradient = 0.5 * (trimmed(partner, across, 2, 0) - trimmed(partner, across, 0, 2))
                flux_term = trimmed(shear_mod, across, 1, 1) * gradient
                total = total + trimmed(0.5 * (trimmed(flux_term, axis_along, 2, 0) - trimmed(flux_term, axis_along, 0, 2)), third_axis, 1, 1)
        components.append(total)
    return jnp.stack(components, axis=-4)


def hat_matrix(offset_cells, fine_count, coarse_count):
    fine_pos = (offset_cells[:, None] + jnp.arange(fine_count, dtype=jnp.int32)[None, :]) * 4
    base_index = fine_pos // 25
    fraction = (fine_pos % 25).astype(jnp.float32) / 25.0
    column = jnp.arange(coarse_count, dtype=jnp.int32)
    first = jnp.where(column[None, None, :] == base_index[:, :, None], 1.0 - fraction[:, :, None], 0.0)
    second = jnp.where(column[None, None, :] == base_index[:, :, None] + 1, fraction[:, :, None], 0.0)
    return first + second


def spread(samples, offset_cells, east_cells, north_cells):
    level_pos = (offset_cells[:, 0:1] + jnp.arange(2, dtype=jnp.int32)[None, :]).astype(jnp.float32) * (4.0 / 25.0)
    upper_level = samples[:, :, :, 0][:, :, :, None]
    lower_level = samples[:, :, :, 1][:, :, :, None]
    vertical = upper_level * (1.0 - level_pos)[:, None, None, :, None, None] + lower_level * level_pos[:, None, None, :, None, None]
    east_matrix = hat_matrix(offset_cells[:, 1], east_cells, samples.shape[-2])
    north_matrix = hat_matrix(offset_cells[:, 2], north_cells, samples.shape[-1])
    eastern = jnp.einsum("kxa,kncjay->kncjxy", east_matrix, vertical, precision=lax.Precision.HIGHEST)
    return jnp.einsum("kncjxa,kya->kncjxy", eastern, north_matrix, precision=lax.Precision.HIGHEST)


def pad_cells(values_in):
    return jnp.pad(values_in, [(0, 0)] * (values_in.ndim - 3) + [(1, 1), (1, 1), (1, 1)])


def reference(disp_now, disp_prev, density, moduli, coarse, block_route, ranges, offsets):
    weights = jnp.array(time_weights, jnp.float32)
    used = coarse[:, :, :CEC * CNC]
    timed_blocks = jnp.einsum("nt,ktpq->knpq", weights, used.reshape(BLOCKS, NT, 6, CEC * CNC), precision=lax.Precision.HIGHEST)
    samples = timed_blocks.reshape(BLOCKS, 2, 3, 2, CEC, CNC)
    shifts = offsets.reshape(TILES * G, 3)[block_route]
    fine_values = spread(samples, shifts, CE, CN)
    placed = jnp.zeros((TILES * G, 2, 3, 2, CE, CN), jnp.float32).at[block_route].set(fine_values)
    incident = placed.reshape(N_GX, N_GY, G, 2, 3, 2, CE, CN).transpose(3, 4, 2, 5, 0, 6, 1, 7).reshape(2, 3, LEV, N_GX * CE, N_GY * CN)
    low_full = jnp.repeat(jnp.repeat(ranges[:, :, 0], CE, axis=0), CN, axis=1)
    high_full = jnp.repeat(jnp.repeat(ranges[:, :, 1], CE, axis=0), CN, axis=1)
    level_ids = jnp.arange(LEV, dtype=jnp.int32)[:, None, None]
    outer_mask = (level_ids < low_full[None]).astype(jnp.float32)
    inner_mask = ((level_ids >= low_full[None]) & (level_ids < high_full[None])).astype(jnp.float32)
    shear_pad = pad_cells(moduli[0])
    lame_pad = pad_cells(moduli[1])

    def applied(values_in):
        return operate(pad_cells(values_in), shear_pad, lame_pad)

    force_first = inner_mask * applied(outer_mask * incident[0]) - outer_mask * applied(inner_mask * incident[0])
    force_second = inner_mask * applied(outer_mask * incident[1]) - outer_mask * applied(inner_mask * incident[1])

    def advance(current, previous, forcing):
        return 2.0 * current - previous + step_square / density * (applied(current) + forcing)

    disp_mid = advance(disp_now, disp_prev, force_first)
    disp_next = advance(disp_mid, disp_now, force_second)
    return incident, disp_mid, disp_next
```

```python
import jax
import jax.numpy as jnp
from jax import lax
from jax.experimental import pallas as pl
from jax.experimental.pallas import tpu as pltpu
from jax.sharding import PartitionSpec as P

step_square = 0.05
time_weights = ((-0.0595, 0.7735, 0.3315, -0.0455), (-0.063756, 0.607068, 0.517132, -0.060444))
NX, NY = 16, 8
LEV, CE, CN = 8, 16, 128
SLABS, PITCH = LEV + 2, 32
COARSE_EAST, COARSE_NORTH = 8, 26
WIDE = 384
MESH = pl.DeviceIdType.MESH
HIGHEST = lax.Precision.HIGHEST
F32 = jnp.float32
START, FORCE_0, FORCE_1, MIDDLE = range(4)
FIELDS = (5, 6, 6, 3)


def iota(shape, dim):
    return lax.broadcasted_iota(jnp.int32, shape, dim)


def dot(a, b):
    return jnp.dot(a, b, precision=HIGHEST, preferred_element_type=F32)


def hat(cells, points):
    return jnp.maximum(25 - jnp.abs(4 * cells - 25 * points), 0).astype(F32) * (1.0 / 25.0)


def kernel(
    now_h, prev_h, dens_h, mod_h, coarse_h, route_s, ranges_s, offs_s,
    inc_h, mid_h, nxt_h,
    prev_v, dens_v, coarse_v, timed_v, turned_v, pay_v, r1, out2, r2, q_v,
    ku0, kum, kup, oi0, oim, oip, md0, mdm, mdp,
    coef, base, inc_v, nxt_v,
    srows, scols, rrows, rcols, rcorn,
    hsend, hrecv, send1, recv1, send2, recv2, local_sem,
):
    gx = lax.axis_index("gx")
    gy = lax.axis_index("gy")

    def x_at(d):
        return lax.rem(gx + (d + NX), NX)

    def y_at(d):
        return lax.rem(gy + (d + NY), NY)

    copies_in = [
        pltpu.make_async_copy(coarse_h, coarse_v, local_sem.at[0]),
        pltpu.make_async_copy(mod_h, ku0.at[0:2, 1:9, 8:24, :], local_sem.at[1]),
        pltpu.make_async_copy(now_h, ku0.at[2:5, 1:9, 8:24, :], local_sem.at[2]),
        pltpu.make_async_copy(prev_h, prev_v, local_sem.at[3]),
        pltpu.make_async_copy(dens_h, dens_v, local_sem.at[4]),
    ]
    for copy in copies_in:
        copy.start()

    barrier = pltpu.get_barrier_semaphore()
    for d in range(1, NX):
        pl.semaphore_signal(barrier, inc=1, device_id=(x_at(d), gy), device_id_type=MESH)
    for d in range(1, NY):
        pl.semaphore_signal(barrier, inc=1, device_id=(gx, y_at(d)), device_id_type=MESH)
    for a in (-1, 1):
        for b in (-1, 1):
            pl.semaphore_signal(barrier, inc=1, device_id=(x_at(a), y_at(b)), device_id_type=MESH)

    copies_in[0].wait()
    for k in range(2):
        for n in range(2):
            row = (k * 2 + n) * 6
            total = None
            for t in range(4):
                term = time_weights[n][t] * coarse_v[k, t * 6:t * 6 + 6, :]
                total = term if total is None else total + term
            timed_v[row:row + 6, :] = total
    timed = timed_v[...]
    for a in range(COARSE_EAST):
        shifted = timed if a == 0 else pltpu.roll(timed, 256 - COARSE_NORTH * a, 1)
        turned_v[a * 24:(a + 1) * 24, :] = shifted[:, :128]
    lane8 = iota((8, 128), 1)
    for k in range(2):
        for tile in range(3):
            joined = None
            for part in range(4):
                piece = turned_v[pl.ds(k * 12 + tile * 4 + part, 8, stride=24), :]
                if part:
                    piece = pltpu.roll(piece, part * 32, 1)
                here = (lane8 >= part * 32) & (lane8 < part * 32 + COARSE_NORTH)
                joined = jnp.where(here, piece, 0.0 if joined is None else joined)
            pay_v[k * 8:(k + 1) * 8, tile * 128:(tile + 1) * 128] = joined

    pl.semaphore_wait(barrier, NX - 1 + NY - 1 + 4)

    own1 = pl.ds(pl.multiple_of(gx * 16, 16), 16)
    stage1 = [
        pltpu.make_async_remote_copy(
            pay_v, r1.at[own1, :], send1.at[d], recv1.at[d],
            device_id=(x_at(d), gy), device_id_type=MESH,
        )
        for d in range(1, NX)
    ]
    for copy in stage1:
        copy.start()
    r1[own1, :] = pay_v[...]

    lane16 = iota((16, 128), 1)
    has_low_x = gx > 0
    has_high_x = gx < NX - 1
    has_low_y = gy > 0
    has_high_y = gy < NY - 1

    def halo_copies(phase):
        count = FIELDS[phase] * 8
        rows_high, rows_low = srows.at[phase, 0, :count], srows.at[phase, 1, :count]
        cols_high, cols_low = scols.at[phase, 0], scols.at[phase, 1]
        plan = [
            (1, 0, rows_high, rrows.at[phase, 0, :count]),
            (-1, 0, rows_low, rrows.at[phase, 1, :count]),
            (0, 1, cols_high, rcols.at[phase, 0]),
            (0, -1, cols_low, rcols.at[phase, 1]),
            (1, 1, scols.at[phase, 0, 8:16], rcorn.at[phase, 0]),
            (1, -1, scols.at[phase, 1, 8:16], rcorn.at[phase, 1]),
            (-1, 1, scols.at[phase, 0, 0:8], rcorn.at[phase, 2]),
            (-1, -1, scols.at[phase, 1, 0:8], rcorn.at[phase, 3]),
        ]
        return [
            pltpu.make_async_remote_copy(
                src, dst, hsend.at[phase, i], hrecv.at[phase, i],
                device_id=(x_at(a), y_at(b)), device_id_type=MESH,
            )
            for i, (a, b, src, dst) in enumerate(plan)
        ]

    halos = [halo_copies(phase) for phase in range(4)]

    def send_edges(phase, pad, first):
        fields = FIELDS[phase]
        flat = pad.reshape(pad.shape[0] * SLABS * PITCH, CN)
        for f in range(fields):
            start = ((first + f) * SLABS + 1) * PITCH + 8
            srows[phase, 0, f * 8:(f + 1) * 8, :] = flat[pl.ds(start + CE - 1, 8, stride=PITCH), :]
            srows[phase, 1, f * 8:(f + 1) * 8, :] = flat[pl.ds(start, 8, stride=PITCH), :]
        halos[phase][0].start()
        halos[phase][1].start()

        def pack(level, carry):
            high, low = carry
            for f in range(fields):
                cells = pad[first + f, level + 1, 8:24, :]
                place = f * 8 + level
                here = lane16 == place
                high = jnp.where(here, pltpu.roll(cells, place + 1, 1), high)
                low = jnp.where(here, pltpu.roll(cells, place, 1), low)
            return high, low

        zero = jnp.zeros((16, 128), F32)
        high, low = lax.fori_loop(0, LEV, pack, (zero, zero))
        scols[phase, 0] = high
        scols[phase, 1] = low
        for copy in halos[phase][2:]:
            copy.start()

    def take_edges(phase, pads, first):
        pad, pad_m, pad_p = pads
        fields = FIELDS[phase]
        for copy in halos[phase]:
            copy.wait_recv()
        flats = [p.reshape(p.shape[0] * SLABS * PITCH, CN) for p in pads]
        sub8 = iota((8, 128), 0)

        def corner(which, row, keep):
            line = jnp.where(keep, rcorn[phase, which, row:row + 1, :], 0.0)
            return jnp.broadcast_to(line, (8, 128))

        corners = (
            (corner(0, 7, has_low_x & has_low_y), corner(1, 7, has_low_x & has_high_y)),
            (corner(2, 0, has_high_x & has_low_y), corner(3, 0, has_high_x & has_high_y)),
        )
        for f in range(fields):
            for side, keep in ((0, has_low_x), (1, has_high_x)):
                start = ((first + f) * SLABS + 1) * PITCH + (7 if side == 0 else 24)
                rows = jnp.where(keep, rrows[phase, side, f * 8:(f + 1) * 8, :], 0.0)
                mine = lane8 == sub8 + f * 8
                left = jnp.sum(jnp.where(mine, corners[side][0], 0.0), axis=1, keepdims=True)
                right = jnp.sum(jnp.where(mine, corners[side][1], 0.0), axis=1, keepdims=True)
                where = pl.ds(start, 8, stride=PITCH)
                flats[0][where, :] = rows
                flats[1][where, :] = jnp.where(lane8 == 0, left, pltpu.roll(rows, 1, 1))
                flats[2][where, :] = jnp.where(lane8 == 127, right, pltpu.roll(rows, 127, 1))
        low = jnp.where(has_low_y, rcols[phase, 0], 0.0)
        high = jnp.where(has_high_y, rcols[phase, 1], 0.0)

        def unpack(level, carry):
            for f in range(fields):
                cells = pad[first + f, level + 1, 8:24, :]
                place = f * 8 + level
                left = pltpu.roll(low, lax.rem(128 - place, 128), 1)
                right = pltpu.roll(high, 127 - place, 1)
                pad_m[first + f, level + 1, 8:24, :] = jnp.where(
                    lane16 == 0, left, pltpu.roll(cells, 1, 1)
                )
                pad_p[first + f, level + 1, 8:24, :] = jnp.where(
                    lane16 == 127, right, pltpu.roll(cells, 127, 1)
                )
            return carry

        lax.fori_loop(0, LEV, unpack, 0)

    blank = jnp.zeros((PITCH, CN), F32)
    for pads, fields in (((ku0, kum, kup), 5), ((oi0, oim, oip), 12), ((md0, mdm, mdp), 3)):

        def clear(f, carry, pads=pads):
            for pad in pads:
                pad[f, 0] = blank
                pad[f, SLABS - 1] = blank
            return carry

        lax.fori_loop(0, fields, clear, 0)

    copies_in[1].wait()
    copies_in[2].wait()
    send_edges(START, ku0, 0)

    tile = gx * NY + gy
    lane256 = iota((1, 256), 1)
    group = lax.div(lane256, 8)
    route = jnp.zeros((1, 256), jnp.int32)
    for x in range(NX):
        for k in range(2):
            route = jnp.where(group == x * 2 + k, route_s[(x * NY + gy) * 2 + k], route)
    row256 = iota((256, 256), 0)
    col256 = iota((256, 256), 1)
    wanted = gx * 32 + lax.div(row256, 8)
    select = jnp.where(
        (wanted == route) & (lax.rem(row256, 8) == lax.rem(col256, 8)), 1.0, 0.0
    ).astype(F32)
    east_rows = []
    for g in range(4):
        cells = iota((16, 256), 0) + offs_s[0, 0, g, 1]
        cols = iota((16, 256), 1)
        weights = hat(cells, lax.rem(cols, 8))
        east_rows.append(jnp.where(lax.rem(lax.div(cols, 8), 4) == g, weights, 0.0))
    east = jnp.concatenate(east_rows, axis=0)
    for g in range(4):
        point = iota((128, 256), 0)
        cell = iota((128, 256), 1)
        north = hat(lax.rem(cell, 128) + offs_s[0, 0, g, 2], lax.rem(point, 32))
        depth = (offs_s[0, 0, g, 0] + lax.div(cell, 128)).astype(F32) * (4.0 / 25.0)
        upright = jnp.where(point < 32, 1.0 - depth, depth)
        keep = (point < 64) & (lax.rem(point, 32) < COARSE_NORTH)
        q_v[g] = jnp.where(keep, north * upright, 0.0)

    for copy in stage1:
        copy.wait_recv()
    out2[...] = dot(select, r1[...])
    stage2 = []
    own2 = pl.ds(pl.multiple_of(gy * 32, 32), 32)
    for d in range(1, NY):
        to = y_at(d)
        stage2.append(
            pltpu.make_async_remote_copy(
                out2.at[pl.ds(pl.multiple_of(to * 32, 32), 32), :], r2.at[own2, :],
                send2.at[d], recv2.at[d], device_id=(gx, to), device_id_type=MESH,
            )
        )
    for copy in stage2:
        copy.start()
    r2[own2, :] = out2[own2, :]

    take_edges(START, (ku0, kum, kup), 0)
    ku = {-1: kum, 0: ku0, 1: kup}
    steps = ((1, 0, 0), (0, 1, 0), (0, 0, 1))

    def moved(d, sign):
        return tuple(sign * s for s in steps[d])

    def prepare(level, carry):
        def get(f, shift):
            dl, de, dn = shift
            return ku[dn][f, level + 1 + dl, 8 + de:24 + de, :]

        mu = get(0, (0, 0, 0))
        stiff = get(1, (0, 0, 0)) + 2.0 * mu
        shear_sides = []
        stiff_sides = []
        for d in range(3):
            for s in range(2):
                shift = moved(d, 1 - 2 * s)
                mu_side = get(0, shift)
                a = 0.5 * (mu + mu_side)
                b = 0.5 * (stiff + (get(1, shift) + 2.0 * mu_side))
                coef[d * 2 + s, level] = a
                coef[6 + d * 2 + s, level] = b
                shear_sides.append(a)
                stiff_sides.append(b)
        for i in range(3):
            total = None
            for d in range(3):
                sides = stiff_sides if d == i else shear_sides
                part = sides[2 * d] + sides[2 * d + 1]
                total = part if total is None else total + part
            coef[12 + i, level] = total
        dens_v[level] = step_square / dens_v[level]
        return carry

    def elastic(level, pads, index):
        cache = {}

        def get(c, shift):
            key = (c, shift)
            if key not in cache:
                dl, de, dn = shift
                cache[key] = pads[dn][index(c), level + 1 + dl, 8 + de:24 + de, :]
            return cache[key]

        kcache = {}

        def modulus(f, shift):
            key = (f, shift)
            if key not in kcache:
                dl, de, dn = shift
                kcache[key] = ku[dn][f, level + 1 + dl, 8 + de:24 + de, :]
            return kcache[key]

        def both(i, si, j, sj):
            a, b = moved(i, si), moved(j, sj)
            return tuple(p + q for p, q in zip(a, b))

        results = []
        for i in range(3):
            total = -coef[12 + i, level] * get(i, (0, 0, 0))
            for d in range(3):
                for s in range(2):
                    at = (6 if d == i else 0) + d * 2 + s
                    total = total + coef[at, level] * get(i, moved(d, 1 - 2 * s))
            mixed = None
            for j in range(3):
                if j == i:
                    continue
                pp = get(j, both(i, 1, j, 1))
                pm = get(j, both(i, 1, j, -1))
                mp = get(j, both(i, -1, j, 1))
                mm = get(j, both(i, -1, j, -1))
                part = (
                    modulus(1, moved(i, 1)) * (pp - pm)
                    - modulus(1, moved(i, -1)) * (mp - mm)
                    + modulus(0, moved(j, 1)) * (pp - mp)
                    - modulus(0, moved(j, -1)) * (pm - mm)
                )
                mixed = part if mixed is None else mixed + part
            results.append(total + 0.25 * mixed)
        return results

    copies_in[4].wait()
    lax.fori_loop(0, LEV, prepare, 0)
    copies_in[3].wait()

    def first_base(level, carry):
        applied = elastic(level, ku, lambda c: 2 + c)
        scale = dens_v[level]
        for c in range(3):
            now = ku0[2 + c, level + 1, 8:24, :]
            base[c, level] = 2.0 * now - prev_v[c, level] + scale * applied[c]
        return carry

    lax.fori_loop(0, LEV, first_base, 0)

    for copy in stage2:
        copy.wait_recv()
    low_level = ranges_s[0, 0, 0]
    high_level = ranges_s[0, 0, 1]
    eastern = dot(east, r2[...])
    for g in range(4):
        pieces = []
        for t in range(3):
            piece = eastern[g * 16:(g + 1) * 16, t * 128:(t + 1) * 128]
            pieces += [piece, pltpu.roll(piece, 64, 1)]
        fine = dot(jnp.concatenate(pieces, axis=0), q_v[g])
        for j in range(2):
            level = 2 * g + j
            outer = (level < low_level).astype(F32)
            inner = ((level >= low_level) & (level < high_level)).astype(F32)
            for n in range(2):
                for c in range(3):
                    p = n * 3 + c
                    cells = fine[p * 16:(p + 1) * 16, j * 128:(j + 1) * 128]
                    inc_v[n, c, level] = cells
                    oi0[n * 6 + c, level + 1, 8:24, :] = outer * cells
                    oi0[n * 6 + 3 + c, level + 1, 8:24, :] = inner * cells
    send_edges(FORCE_0, oi0, 0)
    send_edges(FORCE_1, oi0, 6)
    inc_out = pltpu.make_async_copy(inc_v, inc_h, local_sem.at[5])
    inc_out.start()

    oi = {-1: oim, 0: oi0, 1: oip}
    md = {-1: mdm, 0: md0, 1: mdp}

    def force(level, n):
        inside = (level >= low_level) & (level < high_level)
        which = n * 6 + jnp.where(inside, 0, 3)
        sign = inside.astype(F32) - (level < low_level).astype(F32)
        return sign, elastic(level, oi, lambda c: which + c)

    take_edges(FORCE_0, (oi0, oim, oip), 0)

    def middle(level, carry):
        sign, applied = force(level, 0)
        scale = sign * dens_v[level]
        for c in range(3):
            md0[c, level + 1, 8:24, :] = base[c, level] + scale * applied[c]
        return carry

    lax.fori_loop(0, LEV, middle, 0)
    send_edges(MIDDLE, md0, 0)
    mid_out = pltpu.make_async_copy(md0.at[:, 1:9, 8:24, :], mid_h, local_sem.at[6])
    mid_out.start()

    take_edges(FORCE_1, (oi0, oim, oip), 6)

    def second_base(level, carry):
        sign, applied = force(level, 1)
        scale = sign * dens_v[level]
        for c in range(3):
            mid = md0[c, level + 1, 8:24, :]
            now = ku0[2 + c, level + 1, 8:24, :]
            base[c, level] = 2.0 * mid - now + scale * applied[c]
        return carry

    lax.fori_loop(0, LEV, second_base, 0)
    take_edges(MIDDLE, (md0, mdm, mdp), 0)

    def last(level, carry):
        applied = elastic(level, md, lambda c: c)
        scale = dens_v[level]
        for c in range(3):
            nxt_v[c, level] = base[c, level] + scale * applied[c]
        return carry

    lax.fori_loop(0, LEV, last, 0)
    nxt_out = pltpu.make_async_copy(nxt_v, nxt_h, local_sem.at[7])
    nxt_out.start()
    for copy in stage1 + stage2:
        copy.wait_send()
    for phase in range(4):
        for copy in halos[phase]:
            copy.wait_send()
    inc_out.wait()
    mid_out.wait()
    nxt_out.wait()


def local(disp_now, disp_prev, density, moduli, coarse, block_route, ranges, offsets):
    hbm = pl.BlockSpec(memory_space=pl.ANY)
    smem = pl.BlockSpec(memory_space=pltpu.SMEM)

    def vmem(*shape):
        return pltpu.VMEM(shape, F32)

    dma = pltpu.SemaphoreType.DMA
    return pl.pallas_call(
        kernel,
        out_shape=(
            jax.ShapeDtypeStruct((2, 3, LEV, CE, CN), F32),
            jax.ShapeDtypeStruct((3, LEV, CE, CN), F32),
            jax.ShapeDtypeStruct((3, LEV, CE, CN), F32),
        ),
        in_specs=[hbm] * 5 + [smem] * 3,
        out_specs=(hbm, hbm, hbm),
        scratch_shapes=[
            vmem(3, LEV, CE, CN), vmem(LEV, CE, CN), vmem(2, 24, 256), vmem(24, 256),
            vmem(192, 128), vmem(16, WIDE), vmem(256, WIDE), vmem(256, WIDE), vmem(256, WIDE),
            vmem(4, 128, 256),
            *[vmem(5, SLABS, PITCH, CN)] * 3,
            *[vmem(12, SLABS, PITCH, CN)] * 3,
            *[vmem(3, SLABS, PITCH, CN)] * 3,
            vmem(15, LEV, CE, CN), vmem(3, LEV, CE, CN), vmem(2, 3, LEV, CE, CN),
            vmem(3, LEV, CE, CN),
            vmem(4, 2, 48, 128), vmem(4, 2, 16, 128),
            vmem(4, 2, 48, 128), vmem(4, 2, 16, 128), vmem(4, 4, 8, 128),
            dma((4, 8)), dma((4, 8)), dma((NX,)), dma((NX,)), dma((NY,)), dma((NY,)), dma((8,)),
        ],
        compiler_params=pltpu.CompilerParams(
            collective_id=0, has_side_effects=True, vmem_limit_bytes=48 * 1024 * 1024
        ),
    )(disp_now, disp_prev, density, moduli, coarse, block_route, ranges, offsets)


def solution(mesh):
    return jax.shard_map(
        local,
        mesh=mesh,
        in_specs=(
            P(None, None, "gx", "gy"),
            P(None, None, "gx", "gy"),
            P(None, "gx", "gy"),
            P(None, None, "gx", "gy"),
            P(("gx", "gy"), None, None),
            P(),
            P("gx", "gy", None),
            P("gx", "gy", None, None),
        ),
        out_specs=(
            P(None, None, None, "gx", "gy"),
            P(None, None, "gx", "gy"),
            P(None, None, "gx", "gy"),
        ),
        check_vma=False,
    )
```

```python
import jax
import jax.numpy as jnp
from jax import lax
from jax.experimental import pallas as pl
from jax.experimental.pallas import tpu as pltpu
from jax.sharding import PartitionSpec as P

step_square = 0.05
time_weights = ((-0.0595, 0.7735, 0.3315, -0.0455), (-0.063756, 0.607068, 0.517132, -0.060444))
NX, NY = 16, 8
LEV, CE, CN = 8, 16, 128
SLABS, PITCH = LEV + 2, 32
COARSE_EAST, COARSE_NORTH = 8, 26
MESH = pl.DeviceIdType.MESH
HIGHEST = lax.Precision.HIGHEST
F32 = jnp.float32
START, FORCE_0, FORCE_1, MIDDLE = range(4)


def iota(shape, dim):
    return lax.broadcasted_iota(jnp.int32, shape, dim)


def dot(a, b):
    return jnp.dot(a, b, precision=HIGHEST, preferred_element_type=F32)


def split(x):
    high = x.astype(jnp.bfloat16)
    rest = x - high.astype(F32)
    middle = rest.astype(jnp.bfloat16)
    low = (rest - middle.astype(F32)).astype(jnp.bfloat16)
    return high, middle, low


def dot_exact(whole, x):
    parts = [jnp.dot(whole, part, preferred_element_type=F32) for part in split(x)]
    return (parts[2] + parts[1]) + parts[0]


def kernel(
    now_h, prev_h, dens_h, mod_h, coarse_h, route_h, ranges_h, offs_h,
    inc_v, mid_v, nxt_v,
    route_s, ranges_s, offs_s, prev_v, dens_v, coarse_v, timed_v, turned_v,
    pay_v, r1, out2, r2, pick_v, east_a, east_b, q_v,
    ku0, kum, kup, oi0, oim, oip, md0, mdm, mdp,
    coef, base, srows, scols, rrows, rcols, row_masks,
    hsend, hrecv, send1, recv1, send2, recv2, local_sem,
):
    gx = lax.axis_index("gx")
    gy = lax.axis_index("gy")

    def x_at(d):
        return lax.rem(gx + (d + NX), NX)

    def y_at(d):
        return lax.rem(gy + (d + NY), NY)

    has_x = {1: gx < NX - 1, -1: gx > 0, 0: None}
    has_y = {1: gy < NY - 1, -1: gy > 0, 0: None}

    def has(a, b):
        if a and b:
            return has_x[a] & has_y[b]
        return has_x[a] if a else has_y[b]

    copies_in = [
        pltpu.make_async_copy(coarse_h, coarse_v, local_sem.at[0]),
        pltpu.make_async_copy(mod_h, ku0.at[0:2, 1:9, 8:24, :], local_sem.at[1]),
        pltpu.make_async_copy(now_h, ku0.at[2:5, 1:9, 8:24, :], local_sem.at[2]),
        pltpu.make_async_copy(prev_h, prev_v, local_sem.at[3]),
        pltpu.make_async_copy(dens_h, dens_v, local_sem.at[4]),
        pltpu.make_async_copy(route_h, route_s, local_sem.at[5]),
        pltpu.make_async_copy(ranges_h, ranges_s, local_sem.at[6]),
        pltpu.make_async_copy(offs_h, offs_s, local_sem.at[7]),
    ]
    for at in (0, 5, 6, 7, 1, 2, 3, 4):
        copies_in[at].start()

    barrier = pltpu.get_barrier_semaphore()
    for d in range(1, NX):
        pl.semaphore_signal(barrier, inc=1, device_id=(x_at(d), gy), device_id_type=MESH)
    for d in range(1, NY):
        pl.semaphore_signal(barrier, inc=1, device_id=(gx, y_at(d)), device_id_type=MESH)
    for a in (-1, 1):
        for b in (-1, 1):

            @pl.when(has(a, b))
            def _(a=a, b=b):
                pl.semaphore_signal(
                    barrier, inc=1, device_id=(gx + a, gy + b), device_id_type=MESH
                )

    lane8 = iota((8, 128), 1)
    sub8 = iota((8, 128), 0)
    lane16 = iota((16, 128), 1)

    copies_in[0].wait()
    for n in range(2):
        for k in range(2):
            row = (n * 2 + k) * 6
            total = None
            for t in range(4):
                term = time_weights[n][t] * coarse_v[k, t * 6:t * 6 + 6, :]
                total = term if total is None else total + term
            timed_v[row:row + 6, :] = total
    timed = timed_v[...]
    for a in range(COARSE_EAST):
        shifted = timed if a == 0 else pltpu.roll(timed, 256 - COARSE_NORTH * a, 1)
        turned_v[a * 24:(a + 1) * 24, :] = shifted[:, :128]
    for n in range(2):
        places = [[(n * 2 + k) * 6 + p for p in range(4)] for k in range(2)]
        places.append([(n * 2 + k) * 6 + p for k in range(2) for p in (4, 5)])
        for at, rows in enumerate(places):
            joined = None
            for part, row in enumerate(rows):
                piece = turned_v[pl.ds(row, 8, stride=24), :]
                if part:
                    piece = pltpu.roll(piece, part * 32, 1)
                here = (lane8 >= part * 32) & (lane8 < part * 32 + COARSE_NORTH)
                joined = jnp.where(here, piece, 0.0 if joined is None else joined)
            pay_v[n, at * 8:(at + 1) * 8, :] = joined

    for copy in copies_in[5:]:
        copy.wait()
    low_level = ranges_s[0, 0, 0]
    high_level = ranges_s[0, 0, 1]
    lane256 = iota((1, 256), 1)
    group = lax.div(lane256, 8)
    route = jnp.zeros((1, 256), jnp.int32)
    for x in range(NX):
        for k in range(2):
            route = jnp.where(group == k * NX + x, route_s[(x * NY + gy) * 2 + k], route)
    row256 = iota((256, 256), 0)
    col256 = iota((256, 256), 1)
    wanted = gx * 32 + lax.div(row256, 8)
    pick_v[...] = jnp.where(
        (wanted == route) & (lax.rem(row256, 8) == lax.rem(col256, 8)), 1.0, 0.0
    ).astype(jnp.bfloat16)

    def hat25(cells, points):
        return jnp.maximum(25 - jnp.abs(4 * cells - 25 * points), 0).astype(F32)

    for g in range(4):
        for ref, count in ((east_a, 4), (east_b, 2)):
            shape = (16, count * 64)
            cells = iota(shape, 0) + offs_s[0, 1, 0, g]
            cols = iota(shape, 1)
            weights = hat25(cells, lax.rem(cols, 8))
            mine = lax.rem(lax.div(cols, 8), count) == (g if count == 4 else g // 2)
            ref[g * 16:(g + 1) * 16, :] = jnp.where(mine, weights, 0.0).astype(jnp.bfloat16)
        point = iota((128, 256), 0)
        cell = iota((128, 256), 1)
        north = hat25(lax.rem(cell, 128) + offs_s[0, 2, 0, g], lax.rem(point, 32)) * (1.0 / 625.0)
        depth = (offs_s[0, 0, 0, g] + lax.div(cell, 128)).astype(F32) * (4.0 / 25.0)
        upright = jnp.where(point < 32, 1.0 - depth, depth)
        keep = (point < 64) & (lax.rem(point, 32) < COARSE_NORTH)
        q_v[g] = jnp.where(keep, north * upright, 0.0)

    blank = jnp.zeros((PITCH, CN), F32)
    for pads, fields in (((ku0, kum, kup), 5), ((oi0, oim, oip), 12), ((md0, mdm, mdp), 3)):

        def clear(f, carry, pads=pads):
            for pad in pads:
                pad[f, 0] = blank
                pad[f, SLABS - 1] = blank
            return carry

        lax.fori_loop(0, fields, clear, 0)

    WAYS = ((1, 0), (-1, 0), (1, 1), (1, -1), (-1, 1), (-1, -1), (0, 1), (0, -1))

    def halo_copies(phase):
        rows = 48 if phase == START else 24
        plan = []
        for i, (a, b) in enumerate(WAYS):
            if a:
                src = srows.at[phase, 0 if a > 0 else 1, :rows]
                dst = rrows.at[phase, i, :rows]
            else:
                src = scols.at[phase, i - 6]
                dst = rcols.at[phase, i - 6]
            plan.append(
                pltpu.make_async_remote_copy(
                    src, dst, hsend.at[phase, i], hrecv.at[phase, i],
                    device_id=(gx + a, gy + b), device_id_type=MESH,
                )
            )
        return plan

    halos = [halo_copies(phase) for phase in range(4)]

    def halo_start(phase, which):
        for i in which:

            @pl.when(has(*WAYS[i]))
            def _(i=i):
                halos[phase][i].start()

    def halo_wait(phase):
        for i, (a, b) in enumerate(WAYS):

            @pl.when(has(-a, -b))
            def _(i=i):
                halos[phase][i].wait_recv()

    def pack_rows(phase, flat, first, slab, pitch, fields):
        for f in range(fields):
            start = first + f * slab * pitch
            srows[phase, 0, f * 8:(f + 1) * 8, :] = flat[pl.ds(start + CE - 1, 8, stride=pitch), :]
            srows[phase, 1, f * 8:(f + 1) * 8, :] = flat[pl.ds(start, 8, stride=pitch), :]

    def pack_cols(phase, cells_at, fields, high, low):
        def pack(level, carry):
            high, low = carry
            for f in range(fields):
                cells = cells_at(f, level)
                place = f * 8 + level
                here = lane16 == place
                high = jnp.where(here, pltpu.roll(cells, place + 1, 1), high)
                low = jnp.where(here, pltpu.roll(cells, place, 1), low)
            return high, low

        high, low = lax.fori_loop(0, LEV, pack, (high, low))
        scols[phase, 0] = high
        scols[phase, 1] = low

    def flat_of(pad):
        return pad.reshape(pad.shape[0] * SLABS * PITCH, CN)

    def padded_cells(pad, first):
        return lambda f, level: pad[first + f, level + 1, 8:24, :]

    SIDES = ((0, 2, 3, -1, 7), (1, 4, 5, 1, 24))

    def take_rows(phase, f, masks):
        out = []
        for side, (own, left, right, a, row) in enumerate(SIDES):
            here = slice(f * 8, (f + 1) * 8)
            middle = jnp.where(has(a, 0), rrows[phase, own, here, :], 0.0)
            minus = jnp.where(has(a, -1), rrows[phase, left, here, :], 0.0)
            plus = jnp.where(has(a, 1), rrows[phase, right, here, :], 0.0)
            for oi in range(masks):
                m, lo, hi = middle, minus, plus
                if masks > 1:
                    m = m * row_masks[own, oi]
                    lo = lo * row_masks[left, oi]
                    hi = hi * row_masks[right, oi]
                out.append((
                    side, oi, row, m,
                    pltpu.roll(jnp.where(lane8 == 127, lo, m), 1, 1),
                    pltpu.roll(jnp.where(lane8 == 0, hi, m), 127, 1),
                ))
        return out

    def store_rows(flats, index, row, values):
        where = pl.ds((index * SLABS + 1) * PITCH + row, 8, stride=PITCH)
        for flat, value in zip(flats, values):
            flat[where, :] = value

    def side_cols(phase):
        low = jnp.where(has(0, -1), rcols[phase, 0], 0.0)
        high = jnp.where(has(0, 1), rcols[phase, 1], 0.0)
        return low, high

    def turn(pads, first, fields):
        pad, pad_m, pad_p = pads

        def body(level, carry):
            for f in range(fields):
                cells = pad[first + f, level + 1, 8:24, :]
                pad_m[first + f, level + 1, 8:24, :] = pltpu.roll(cells, 1, 1)
                pad_p[first + f, level + 1, 8:24, :] = pltpu.roll(cells, 127, 1)
            return carry

        lax.fori_loop(0, LEV, body, 0)

    def take_edges(phase, pads, fields):
        _, pad_m, pad_p = pads
        flats = [flat_of(p) for p in pads]
        for f in range(fields):
            for _, _, row, m, lo, hi in take_rows(phase, f, 1):
                store_rows(flats, f, row, (m, lo, hi))
        low, high = side_cols(phase)

        def body(level, carry):
            for f in range(fields):
                place = f * 8 + level
                left = pltpu.roll(low, lax.rem(128 - place, 128), 1)
                right = pltpu.roll(high, 127 - place, 1)
                at_m = pad_m[f, level + 1, 8:24, :]
                at_p = pad_p[f, level + 1, 8:24, :]
                pad_m[f, level + 1, 8:24, :] = jnp.where(lane16 == 0, left, at_m)
                pad_p[f, level + 1, 8:24, :] = jnp.where(lane16 == 127, right, at_p)
            return carry

        lax.fori_loop(0, LEV, body, 0)

    copies_in[1].wait()
    copies_in[2].wait()
    range_rows = jnp.where(sub8 == 0, low_level, high_level).astype(F32)
    pack_rows(START, flat_of(ku0), PITCH + 8, SLABS, PITCH, 5)
    for side in range(2):
        srows[START, side, 40:48, :] = range_rows
    range_cols = jnp.where(lane16 == 40, low_level, high_level).astype(F32)
    pack_cols(START, padded_cells(ku0, 0), 5, range_cols, range_cols)
    turn((ku0, kum, kup), 0, 5)

    diagonal = (has_x[1].astype(jnp.int32) + has_x[-1].astype(jnp.int32)) * (
        has_y[1].astype(jnp.int32) + has_y[-1].astype(jnp.int32)
    )
    pl.semaphore_wait(barrier, NX - 1 + NY - 1 + diagonal)

    stage1 = [
        [
            pltpu.make_async_remote_copy(
                pay_v.at[n], r1.at[n, gx], send1.at[n, d], recv1.at[n, d],
                device_id=(x_at(d), gy), device_id_type=MESH,
            )
            for d in range(1, NX)
        ]
        for n in range(2)
    ]
    stage2 = [[], []]

    def line_start(n):
        for copy in stage1[n]:
            copy.start()
        r1[n, gx] = pay_v[n]

    def slots_start(n):
        for copy in stage1[n]:
            copy.wait_recv()
        held = r1[n]
        first = jnp.swapaxes(held[:, 0:16, :].reshape(NX, 2, 8, 128), 0, 1).reshape(256, 128)
        second = held[:, 16:24, :].reshape(128, 128)
        second = jnp.concatenate([second, pltpu.roll(second, 64, 1)], axis=0)
        found = dot_exact(pick_v[...], jnp.concatenate([first, second], axis=1))
        out2[n, :, 0:32, :] = found[:, :128].reshape(NY, 32, 128)
        folded = found[:, 128:].reshape(NY, 2, 2, 8, 128)
        even = folded[:, :, 0].reshape(128, 128)
        odd = pltpu.roll(folded[:, :, 1].reshape(128, 128), 64, 1)
        lanes = iota((128, 128), 1)
        out2[n, :, 32:48, :] = jnp.where(lanes < 64, even, odd).reshape(NY, 16, 128)
        for d in range(1, NY):
            to = y_at(d)
            stage2[n].append(
                pltpu.make_async_remote_copy(
                    out2.at[n, to], r2.at[n, gy], send2.at[n, d], recv2.at[n, d],
                    device_id=(gx, to), device_id_type=MESH,
                )
            )
        for copy in stage2[n]:
            copy.start()
        r2[n, gy] = out2[n, gy]

    line_start(0)
    line_start(1)
    halo_start(START, range(8))
    slots_start(0)
    slots_start(1)

    halo_wait(START)
    take_edges(START, (ku0, kum, kup), 5)
    level8 = sub8.astype(F32)
    for i in range(6):
        low = rrows[START, i, 40:41, :]
        high = rrows[START, i, 41:42, :]
        row_masks[i, 0] = jnp.where(level8 < low, 1.0, 0.0)
        row_masks[i, 1] = jnp.where((level8 >= low) & (level8 < high), 1.0, 0.0)
    ku = {-1: kum, 0: ku0, 1: kup}
    steps = ((1, 0, 0), (0, 1, 0), (0, 0, 1))

    def moved(d, sign):
        return tuple(sign * s for s in steps[d])

    def prepare(level, carry):
        def get(f, shift):
            dl, de, dn = shift
            return ku[dn][f, level + 1 + dl, 8 + de:24 + de, :]

        mu = get(0, (0, 0, 0))
        stiff = get(1, (0, 0, 0)) + 2.0 * mu
        shear_sides = []
        stiff_sides = []
        for d in range(3):
            for s in range(2):
                shift = moved(d, 1 - 2 * s)
                mu_side = get(0, shift)
                a = 0.5 * (mu + mu_side)
                b = 0.5 * (stiff + (get(1, shift) + 2.0 * mu_side))
                coef[d * 2 + s, level] = a
                coef[6 + d * 2 + s, level] = b
                shear_sides.append(a)
                stiff_sides.append(b)
        for i in range(3):
            total = None
            for d in range(3):
                sides = stiff_sides if d == i else shear_sides
                part = sides[2 * d] + sides[2 * d + 1]
                total = part if total is None else total + part
            coef[12 + i, level] = total
        dens_v[level] = step_square / dens_v[level]
        return carry

    def elastic(level, pads, index):
        cache = {}

        def get(c, shift):
            key = (c, shift)
            if key not in cache:
                dl, de, dn = shift
                cache[key] = pads[dn][index(c), level + 1 + dl, 8 + de:24 + de, :]
            return cache[key]

        kcache = {}

        def modulus(f, shift):
            key = (f, shift)
            if key not in kcache:
                dl, de, dn = shift
                kcache[key] = ku[dn][f, level + 1 + dl, 8 + de:24 + de, :]
            return kcache[key]

        def both(i, si, j, sj):
            a, b = moved(i, si), moved(j, sj)
            return tuple(p + q for p, q in zip(a, b))

        results = []
        for i in range(3):
            total = -coef[12 + i, level] * get(i, (0, 0, 0))
            for d in range(3):
                for s in range(2):
                    at = (6 if d == i else 0) + d * 2 + s
                    total = total + coef[at, level] * get(i, moved(d, 1 - 2 * s))
            mixed = None
            for j in range(3):
                if j == i:
                    continue
                pp = get(j, both(i, 1, j, 1))
                pm = get(j, both(i, 1, j, -1))
                mp = get(j, both(i, -1, j, 1))
                mm = get(j, both(i, -1, j, -1))
                part = (
                    modulus(1, moved(i, 1)) * (pp - pm)
                    - modulus(1, moved(i, -1)) * (mp - mm)
                    + modulus(0, moved(j, 1)) * (pp - mp)
                    - modulus(0, moved(j, -1)) * (pm - mm)
                )
                mixed = part if mixed is None else mixed + part
            results.append(total + 0.25 * mixed)
        return results

    copies_in[4].wait()
    lax.fori_loop(0, LEV, prepare, 0)
    copies_in[3].wait()

    def first_base(level, carry):
        applied = elastic(level, ku, lambda c: 2 + c)
        scale = dens_v[level]
        for c in range(3):
            now = ku0[2 + c, level + 1, 8:24, :]
            base[c, level] = 2.0 * now - prev_v[c, level] + scale * applied[c]
        return carry

    lax.fori_loop(0, LEV, first_base, 0)

    def incident(n):
        for copy in stage2[n]:
            copy.wait_recv()
        got = r2[n]
        eastern_a = dot_exact(east_a[...], got[:, 0:32, :].reshape(256, 128))
        eastern_b = dot_exact(east_b[...], got[:, 32:48, :].reshape(128, 128))
        for g in range(4):
            piece_a = eastern_a[g * 16:(g + 1) * 16]
            piece_b = eastern_b[g * 16:(g + 1) * 16]
            if g % 2:
                piece_b = pltpu.roll(piece_b, 64, 1)
            pieces = [piece_a, pltpu.roll(piece_a, 64, 1), piece_b]
            fine = dot(jnp.concatenate(pieces, axis=0), q_v[g])
            for j in range(2):
                for c in range(3):
                    inc_v[n, c, 2 * g + j] = fine[c * 16:(c + 1) * 16, j * 128:(j + 1) * 128]
        phase = FORCE_0 + n
        flat = inc_v.reshape(6 * LEV * CE, CN)
        pack_rows(phase, flat, n * 3 * LEV * CE, LEV, CE, 3)
        halo_start(phase, range(6))
        zero = jnp.zeros((16, 128), F32)
        pack_cols(phase, lambda f, level: inc_v[n, f, level], 3, zero, zero)
        halo_start(phase, (6, 7))

    def mask_inside(n):
        def body(level, carry):
            outer = (level < low_level).astype(F32)
            inner = ((level >= low_level) & (level < high_level)).astype(F32)
            for c in range(3):
                cells = inc_v[n, c, level]
                values = (cells, pltpu.roll(cells, 1, 1), pltpu.roll(cells, 127, 1))
                for pad, value in zip((oi0, oim, oip), values):
                    pad[n * 6 + c, level + 1, 8:24, :] = outer * value
                    pad[n * 6 + 3 + c, level + 1, 8:24, :] = inner * value
            return carry

        lax.fori_loop(0, LEV, body, 0)

    def take_masked(n):
        phase = FORCE_0 + n
        halo_wait(phase)
        flats = [flat_of(p) for p in (oi0, oim, oip)]
        for c in range(3):
            for _, oi, row, m, lo, hi in take_rows(phase, c, 2):
                store_rows(flats, n * 6 + oi * 3 + c, row, (m, lo, hi))
        low, high = side_cols(phase)
        bounds = []
        for side in range(2):
            got = rcols[START, side]
            bounds.append([
                jnp.broadcast_to(got[:, 40 + b:41 + b], (16, 128)) for b in range(2)
            ])

        def body(level, carry):
            here = level.astype(F32)
            outer = [here < bounds[side][0] for side in range(2)]
            inner = [(here >= bounds[side][0]) & (here < bounds[side][1]) for side in range(2)]
            for c in range(3):
                place = c * 8 + level
                left = pltpu.roll(low, lax.rem(128 - place, 128), 1)
                right = pltpu.roll(high, 127 - place, 1)
                for oi, masks in ((0, outer), (1, inner)):
                    at = n * 6 + oi * 3 + c
                    at_m = oim[at, level + 1, 8:24, :]
                    at_p = oip[at, level + 1, 8:24, :]
                    new_m = jnp.where(masks[0], left, 0.0)
                    new_p = jnp.where(masks[1], right, 0.0)
                    oim[at, level + 1, 8:24, :] = jnp.where(lane16 == 0, new_m, at_m)
                    oip[at, level + 1, 8:24, :] = jnp.where(lane16 == 127, new_p, at_p)
            return carry

        lax.fori_loop(0, LEV, body, 0)

    incident(0)
    mask_inside(0)
    incident(1)

    oi = {-1: oim, 0: oi0, 1: oip}
    md = {-1: mdm, 0: md0, 1: mdp}

    def force(level, n):
        inside = (level >= low_level) & (level < high_level)
        which = n * 6 + jnp.where(inside, 0, 3)
        sign = inside.astype(F32) - (level < low_level).astype(F32)
        return sign, elastic(level, oi, lambda c: which + c)

    take_masked(0)

    def middle(level, carry):
        sign, applied = force(level, 0)
        scale = sign * dens_v[level]
        for c in range(3):
            cells = base[c, level] + scale * applied[c]
            md0[c, level + 1, 8:24, :] = cells
            mid_v[c, level] = cells
        return carry

    lax.fori_loop(0, LEV, middle, 0)
    pack_rows(MIDDLE, flat_of(md0), PITCH + 8, SLABS, PITCH, 3)
    halo_start(MIDDLE, range(6))
    zero = jnp.zeros((16, 128), F32)
    pack_cols(MIDDLE, padded_cells(md0, 0), 3, zero, zero)
    halo_start(MIDDLE, (6, 7))
    mask_inside(1)
    turn((md0, mdm, mdp), 0, 3)
    take_masked(1)

    def second_base(level, carry):
        sign, applied = force(level, 1)
        scale = sign * dens_v[level]
        for c in range(3):
            mid = md0[c, level + 1, 8:24, :]
            now = ku0[2 + c, level + 1, 8:24, :]
            base[c, level] = 2.0 * mid - now + scale * applied[c]
        return carry

    lax.fori_loop(0, LEV, second_base, 0)
    halo_wait(MIDDLE)
    take_edges(MIDDLE, (md0, mdm, mdp), 3)

    def last(level, carry):
        applied = elastic(level, md, lambda c: c)
        scale = dens_v[level]
        for c in range(3):
            nxt_v[c, level] = base[c, level] + scale * applied[c]
        return carry

    lax.fori_loop(0, LEV, last, 0)
    for n in range(2):
        for copy in stage1[n] + stage2[n]:
            copy.wait_send()
    for phase in range(4):
        for i, (a, b) in enumerate(WAYS):

            @pl.when(has(a, b))
            def _(i=i, phase=phase):
                halos[phase][i].wait_send()


def hand_out(inc_v, mid_v, nxt_v, inc_h, mid_h, nxt_h, sems):
    copies = [
        pltpu.make_async_copy(src, dst, sems.at[i])
        for i, (src, dst) in enumerate(((inc_v, inc_h), (mid_v, mid_h), (nxt_v, nxt_h)))
    ]
    for copy in copies:
        copy.start()
    for copy in copies:
        copy.wait()


def local(disp_now, disp_prev, density, moduli, coarse, block_route, ranges, offsets):
    hbm = pl.BlockSpec(memory_space=pl.ANY)
    on_chip = pl.BlockSpec(memory_space=pltpu.VMEM)

    def vmem(*shape):
        return pltpu.VMEM(shape, F32)

    dma = pltpu.SemaphoreType.DMA
    outs = (
        jax.ShapeDtypeStruct((2, 3, LEV, CE, CN), F32),
        jax.ShapeDtypeStruct((3, LEV, CE, CN), F32),
        jax.ShapeDtypeStruct((3, LEV, CE, CN), F32),
    )
    args = (
        disp_now, disp_prev, density, moduli, coarse, block_route, ranges,
        offsets.transpose(0, 3, 1, 2),
    )
    results = pl.pallas_call(
        kernel,
        out_shape=outs,
        in_specs=[hbm] * 8,
        out_specs=(on_chip,) * 3,
        scratch_shapes=[
            pltpu.SMEM((256,), jnp.int32), pltpu.SMEM((1, 1, 2), jnp.int32),
            pltpu.SMEM((1, 3, 1, 4), jnp.int32),
            vmem(3, LEV, CE, CN), vmem(LEV, CE, CN), vmem(2, 24, 256), vmem(24, 256),
            vmem(192, 128), vmem(2, 24, 128), vmem(2, NX, 24, 128), vmem(2, NY, 48, 128),
            vmem(2, NY, 48, 128), pltpu.VMEM((256, 256), jnp.bfloat16),
            pltpu.VMEM((64, 256), jnp.bfloat16), pltpu.VMEM((64, 128), jnp.bfloat16),
            vmem(4, 128, 256),
            *[vmem(5, SLABS, PITCH, CN)] * 3,
            *[vmem(12, SLABS, PITCH, CN)] * 3,
            *[vmem(3, SLABS, PITCH, CN)] * 3,
            vmem(15, LEV, CE, CN), vmem(3, LEV, CE, CN),
            vmem(4, 2, 48, 128), vmem(4, 2, 16, 128),
            vmem(4, 6, 48, 128), vmem(4, 2, 16, 128), vmem(6, 2, 8, 128),
            dma((4, 8)), dma((4, 8)), dma((2, NX)), dma((2, NX)), dma((2, NY)), dma((2, NY)),
            dma((8,)),
        ],
        compiler_params=pltpu.CompilerParams(
            collective_id=0, has_side_effects=True, vmem_limit_bytes=48 * 1024 * 1024
        ),
    )(*[pltpu.with_memory_space_constraint(v, pltpu.HBM) for v in args])
    return pl.pallas_call(
        hand_out,
        out_shape=outs,
        in_specs=[on_chip] * 3,
        out_specs=(hbm, hbm, hbm),
        scratch_shapes=[dma((3,))],
        compiler_params=pltpu.CompilerParams(vmem_limit_bytes=4 * 1024 * 1024),
    )(*results)


def solution(mesh):
    return jax.shard_map(
        local,
        mesh=mesh,
        in_specs=(
            P(None, None, "gx", "gy"),
            P(None, None, "gx", "gy"),
            P(None, "gx", "gy"),
            P(None, None, "gx", "gy"),
            P(("gx", "gy"), None, None),
            P(),
            P("gx", "gy", None),
            P("gx", "gy", None, None),
        ),
        out_specs=(
            P(None, None, None, "gx", "gy"),
            P(None, None, "gx", "gy"),
            P(None, None, "gx", "gy"),
        ),
        check_vma=False,
    )
```

```python
import jax
import jax.numpy as jnp
from jax import lax
from jax.experimental import pallas as pl
from jax.experimental.pallas import tpu as pltpu
from jax.sharding import PartitionSpec as P

step_square = 0.05
time_weights = ((-0.0595, 0.7735, 0.3315, -0.0455), (-0.063756, 0.607068, 0.517132, -0.060444))
NX, NY = 16, 8
LEV, CE, CN = 8, 16, 128
SLABS, PITCH = LEV + 2, 32
COARSE_EAST, COARSE_NORTH = 8, 26
MESH = pl.DeviceIdType.MESH
FAR_X = (10, 9, 11, 6, 14, 7, 5, 13, 15, 8, 2, 4, 12, 1, 3)
FAR_Y = (4, 3, 5, 2, 6, 1, 7)
F32 = jnp.float32
START, FORCE_0, FORCE_1, MIDDLE = range(4)


def iota(shape, dim):
    return lax.broadcasted_iota(jnp.int32, shape, dim)


def split(x):
    high = x.astype(jnp.bfloat16)
    rest = x - high.astype(F32)
    middle = rest.astype(jnp.bfloat16)
    low = (rest - middle.astype(F32)).astype(jnp.bfloat16)
    return high, middle, low


def dot_exact(whole, x):
    parts = [jnp.dot(whole, part, preferred_element_type=F32) for part in split(x)]
    return (parts[2] + parts[1]) + parts[0]


def kernel(
    now_h, prev_h, dens_h, mod_h, coarse_h, route_h, ranges_h, offs_h,
    inc_v, mid_v, nxt_v,
    route_s, ranges_s, offs_s, prev_v, dens_v, coarse_v, timed_v, turned_v,
    found_s, pay_v, r1_0, r1_1, out2, r2, east_a, east_b, q_high, q_low,
    ku0, kum, kup, oi0, oim, oip, md0, mdm, mdp,
    coef, base, srows, scols, rrows, rcols, row_masks,
    hsend, hrecv, send1, recv1, send2, recv2, local_sem,
):
    gx = lax.axis_index("gx")
    gy = lax.axis_index("gy")

    def x_at(d):
        return lax.rem(gx + (d + NX), NX)

    def y_at(d):
        return lax.rem(gy + (d + NY), NY)

    has_x = {1: gx < NX - 1, -1: gx > 0, 0: None}
    has_y = {1: gy < NY - 1, -1: gy > 0, 0: None}

    def has(a, b):
        if a and b:
            return has_x[a] & has_y[b]
        return has_x[a] if a else has_y[b]

    copies_in = [
        pltpu.make_async_copy(coarse_h, coarse_v, local_sem.at[0]),
        pltpu.make_async_copy(mod_h, ku0.at[3:5, 1:9, 8:24, :], local_sem.at[1]),
        pltpu.make_async_copy(now_h, ku0.at[0:3, 1:9, 8:24, :], local_sem.at[2]),
        pltpu.make_async_copy(prev_h, prev_v, local_sem.at[3]),
        pltpu.make_async_copy(dens_h, dens_v, local_sem.at[4]),
        pltpu.make_async_copy(route_h, route_s, local_sem.at[5]),
        pltpu.make_async_copy(ranges_h, ranges_s, local_sem.at[6]),
        pltpu.make_async_copy(offs_h, offs_s, local_sem.at[7]),
    ]
    for at in (0, 5, 6, 7, 1, 2, 3, 4):
        copies_in[at].start()

    barrier = pltpu.get_barrier_semaphore()
    for d in range(1, NX):
        pl.semaphore_signal(barrier, inc=1, device_id=(x_at(d), gy), device_id_type=MESH)
    for d in range(1, NY):
        pl.semaphore_signal(barrier, inc=1, device_id=(gx, y_at(d)), device_id_type=MESH)
    for a in (-1, 1):
        for b in (-1, 1):

            @pl.when(has(a, b))
            def _(a=a, b=b):
                pl.semaphore_signal(
                    barrier, inc=1, device_id=(gx + a, gy + b), device_id_type=MESH
                )

    lane8 = iota((8, 128), 1)
    sub8 = iota((8, 128), 0)
    lane16 = iota((16, 128), 1)

    copies_in[0].wait()
    for n in range(2):
        for k in range(2):
            row = (n * 2 + k) * 6
            total = None
            for t in range(4):
                term = time_weights[n][t] * coarse_v[k, t * 6:t * 6 + 6, :]
                total = term if total is None else total + term
            timed_v[row:row + 6, :] = total
    timed = timed_v[...]
    for a in range(COARSE_EAST):
        shifted = timed if a == 0 else pltpu.roll(timed, 256 - COARSE_NORTH * a, 1)
        turned_v[a * 24:(a + 1) * 24, :] = shifted[:, :128]
    for n in range(2):
        places = [[(n * 2 + k) * 6 + p for p in range(4)] for k in range(2)]
        places.append([(n * 2 + k) * 6 + p for k in range(2) for p in (4, 5)])
        for at, rows in enumerate(places):
            joined = None
            for part, row in enumerate(rows):
                piece = turned_v[pl.ds(row, 8, stride=24), :]
                if part:
                    piece = pltpu.roll(piece, part * 32, 1)
                here = (lane8 >= part * 32) & (lane8 < part * 32 + COARSE_NORTH)
                joined = jnp.where(here, piece, 0.0 if joined is None else joined)
            pay_v[n, at] = joined

    for copy in copies_in[5:]:
        copy.wait()
    low_level = ranges_s[0, 0, 0]
    high_level = ranges_s[0, 0, 1]
    blank = jnp.zeros((PITCH, CN), F32)
    for pads, fields in (((ku0, kum, kup), 5), ((oi0, oim, oip), 12), ((md0, mdm, mdp), 3)):

        def clear(f, carry, pads=pads):
            for pad in pads:
                pad[f, 0] = blank
                pad[f, SLABS - 1] = blank
            return carry

        lax.fori_loop(0, fields, clear, 0)

    WAYS = ((1, 1), (1, -1), (-1, 1), (-1, -1), (1, 0), (-1, 0), (0, 1), (0, -1))

    def slot_of(f):
        return f if f < 3 else f + 1

    def halo_copies(phase):
        plan = []
        for i, (a, b) in enumerate(WAYS):
            rows = 24
            if phase == START:
                rows = 32 if b else 48
            if a:
                src = srows.at[phase, 0 if a > 0 else 1, :rows]
                dst = rrows.at[phase, i, :rows]
            else:
                src = scols.at[phase, i - 6]
                dst = rcols.at[phase, i - 6]
            plan.append(
                pltpu.make_async_remote_copy(
                    src, dst, hsend.at[phase, i], hrecv.at[phase, i],
                    device_id=(gx + a, gy + b), device_id_type=MESH,
                )
            )
        return plan

    halos = [halo_copies(phase) for phase in range(4)]

    def halo_start(phase, which):
        for i in which:

            @pl.when(has(*WAYS[i]))
            def _(i=i):
                halos[phase][i].start()

    def halo_wait(phase):
        for i, (a, b) in enumerate(WAYS):

            @pl.when(has(-a, -b))
            def _(i=i):
                halos[phase][i].wait_recv()

    def halo_sent(phase):
        for i, (a, b) in enumerate(WAYS):

            @pl.when(has(a, b))
            def _(i=i):
                halos[phase][i].wait_send()

    def pack_rows(phase, flat, first, slab, pitch, fields):
        for f in range(fields):
            start = first + f * slab * pitch
            at = slot_of(f) * 8
            srows[phase, 0, at:at + 8, :] = flat[pl.ds(start + CE - 1, 8, stride=pitch), :]
            srows[phase, 1, at:at + 8, :] = flat[pl.ds(start, 8, stride=pitch), :]

    def pack_cols(phase, cells_at, fields, high, low):
        def pack(level, carry):
            high, low = carry
            for f in range(fields):
                cells = cells_at(f, level)
                place = slot_of(f) * 8 + level
                here = lane16 == place
                high = jnp.where(here, pltpu.roll(cells, place + 1, 1), high)
                low = jnp.where(here, pltpu.roll(cells, place, 1), low)
            return high, low

        for level in range(LEV):
            high, low = pack(level, (high, low))
        scols[phase, 0] = high
        scols[phase, 1] = low

    def flat_of(pad):
        return pad.reshape(pad.shape[0] * SLABS * PITCH, CN)

    def padded_cells(pad, first):
        return lambda f, level: pad[first + f, level + 1, 8:24, :]

    SIDES = ((4, 0, 1, -1, 7), (5, 2, 3, 1, 24))

    def take_rows(phase, f, masks):
        out = []
        for side, (own, left, right, a, row) in enumerate(SIDES):
            here = slice(slot_of(f) * 8, slot_of(f) * 8 + 8)
            middle = jnp.where(has(a, 0), rrows[phase, own, here, :], 0.0)
            minus = plus = jnp.zeros((8, 128), F32)
            if f < 3:
                minus = jnp.where(has(a, -1), rrows[phase, left, here, :], 0.0)
                plus = jnp.where(has(a, 1), rrows[phase, right, here, :], 0.0)
            for oi in range(masks):
                m, lo, hi = middle, minus, plus
                if masks > 1:
                    m = m * row_masks[own, oi]
                    lo = lo * row_masks[left, oi]
                    hi = hi * row_masks[right, oi]
                out.append((
                    side, oi, row, m,
                    pltpu.roll(jnp.where(lane8 == 127, lo, m), 1, 1),
                    pltpu.roll(jnp.where(lane8 == 0, hi, m), 127, 1),
                ))
        return out

    def store_rows(flats, index, row, values):
        where = pl.ds((index * SLABS + 1) * PITCH + row, 8, stride=PITCH)
        for flat, value in zip(flats, values):
            flat[where, :] = value

    def side_cols(phase):
        low = jnp.where(has(0, -1), rcols[phase, 0], 0.0)
        high = jnp.where(has(0, 1), rcols[phase, 1], 0.0)
        return low, high

    def turn(pads, first, fields):
        pad, pad_m, pad_p = pads

        def body(level, carry):
            for f in range(fields):
                cells = pad[first + f, level + 1, 8:24, :]
                pad_m[first + f, level + 1, 8:24, :] = pltpu.roll(cells, 1, 1)
                pad_p[first + f, level + 1, 8:24, :] = pltpu.roll(cells, 127, 1)
            return carry

        for level in range(LEV):
            body(level, 0)

    def take_edges(phase, pads, fields):
        _, pad_m, pad_p = pads
        flats = [flat_of(p) for p in pads]
        for f in range(fields):
            for _, _, row, m, lo, hi in take_rows(phase, f, 1):
                store_rows(flats, f, row, (m, lo, hi))
        low, high = side_cols(phase)

        def body(level, carry):
            for f in range(fields):
                place = slot_of(f) * 8 + level
                left = pltpu.roll(low, (128 - place) % 128, 1)
                right = pltpu.roll(high, 127 - place, 1)
                at_m = pad_m[f, level + 1, 8:24, :]
                at_p = pad_p[f, level + 1, 8:24, :]
                pad_m[f, level + 1, 8:24, :] = jnp.where(lane16 == 0, left, at_m)
                pad_p[f, level + 1, 8:24, :] = jnp.where(lane16 == 127, right, at_p)
            return carry

        for level in range(LEV):
            body(level, 0)

    copies_in[1].wait()
    copies_in[2].wait()
    range_rows = jnp.where(sub8 == 0, low_level, high_level).astype(F32)
    pack_rows(START, flat_of(ku0), PITCH + 8, SLABS, PITCH, 5)
    for side in range(2):
        srows[START, side, 24:32, :] = range_rows
    range_cols = jnp.where(lane16 == 24, low_level, high_level).astype(F32)
    pack_cols(START, padded_cells(ku0, 0), 5, range_cols, range_cols)
    turn((ku0, kum, kup), 0, 5)

    diagonal = (has_x[1].astype(jnp.int32) + has_x[-1].astype(jnp.int32)) * (
        has_y[1].astype(jnp.int32) + has_y[-1].astype(jnp.int32)
    )
    pl.semaphore_wait(barrier, NX - 1 + NY - 1 + diagonal)

    r1 = (r1_0, r1_1)

    stage1 = [
        [
            pltpu.make_async_remote_copy(
                pay_v.at[n], r1[n].at[pl.ds(gx * 3, 3)], send1.at[n, d], recv1.at[n, d],
                device_id=(x_at(d), gy), device_id_type=MESH,
            )
            for d in FAR_X
        ]
        for n in range(2)
    ]
    stage2 = [[], []]

    def line_start(n):
        for copy in stage1[n]:
            copy.start()
        r1[n][pl.ds(gx * 3, 3)] = pay_v[n]

    lane_half = lane8 < 64

    def slots_start(n):
        for copy in stage1[n]:
            copy.wait_recv()

        def fill(to, carry):
            halves = []
            for g in range(4):
                place = found_s[to * 4 + g]
                at = jnp.clip(place - 1, 0, 3 * NX - 2)
                k = lax.rem(at, 3)
                first = r1[n][at]
                second = r1[n][at - k + 2]
                second = pltpu.roll(second, 64 * lax.rem(k + g, 2), 1)
                out2[n, to, g * 8:(g + 1) * 8, :] = jnp.where(place > 0, first, 0.0)
                halves.append(jnp.where(place > 0, second, 0.0))
            for h in range(2):
                joined = jnp.where(lane_half, halves[2 * h], halves[2 * h + 1])
                out2[n, to, 32 + h * 8:40 + h * 8, :] = joined
            return carry

        for d in FAR_Y + (0,):
            to = y_at(d)
            fill(to, 0)
            if d == 0:
                continue
            copy = pltpu.make_async_remote_copy(
                out2.at[n, to], r2.at[n, gy], send2.at[n, d], recv2.at[n, d],
                device_id=(gx, to), device_id_type=MESH,
            )
            copy.start()
            stage2[n].append(copy)
        r2[n, gy] = out2[n, gy]

    line_start(0)
    halo_start(START, range(8))
    line_start(1)

    def find(slot, carry):
        place = jnp.int32(0)
        for x in range(NX):
            for k in range(2):
                named = route_s[(x * NY + gy) * 2 + k] == gx * 32 + slot
                place = jnp.maximum(place, jnp.where(named, 1 + 3 * x + k, 0))
        found_s[slot] = place
        return carry

    lax.fori_loop(0, NY * 4, find, 0)

    def hat25(cells, points):
        return jnp.maximum(25 - jnp.abs(4 * cells - 25 * points), 0).astype(F32)

    for g in range(4):
        for ref, count in ((east_a, 4), (east_b, 2)):
            shape = (16, count * 8)
            cells = iota(shape, 0) + offs_s[0, 1, 0, g]
            cols = iota(shape, 1)
            weights = hat25(cells, lax.rem(cols, 8))
            mine = lax.div(cols, 8) == (g if count == 4 else g // 2)
            ref[g * 16:(g + 1) * 16, :] = jnp.where(mine, weights, 0.0).astype(jnp.bfloat16)
        point = iota((128, 256), 0)
        cell = iota((128, 256), 1)
        north = hat25(lax.rem(cell, 128) + offs_s[0, 2, 0, g], lax.rem(point, 32)) * (1.0 / 625.0)
        depth = (offs_s[0, 0, 0, g] + lax.div(cell, 128)).astype(F32) * (4.0 / 25.0)
        upright = jnp.where(point < 32, 1.0 - depth, depth)
        keep = (point < 64) & (lax.rem(point, 32) < COARSE_NORTH)
        weights = jnp.where(keep, north * upright, 0.0)
        high = weights.astype(jnp.bfloat16)
        q_high[g] = high
        q_low[g] = (weights - high.astype(F32)).astype(jnp.bfloat16)

    slots_start(0)

    halo_wait(START)
    take_edges(START, (ku0, kum, kup), 5)
    level8 = sub8.astype(F32)
    for i in range(6):
        low = rrows[START, i, 24:25, :]
        high = rrows[START, i, 25:26, :]
        row_masks[i, 0] = jnp.where(level8 < low, 1.0, 0.0)
        row_masks[i, 1] = jnp.where((level8 >= low) & (level8 < high), 1.0, 0.0)
    ku = {-1: kum, 0: ku0, 1: kup}
    steps = ((1, 0, 0), (0, 1, 0), (0, 0, 1))

    def moved(d, sign):
        return tuple(sign * s for s in steps[d])

    def prepare(level, carry):
        def get(f, shift):
            dl, de, dn = shift
            return ku[dn][f, level + 1 + dl, 8 + de:24 + de, :]

        mu = get(3, (0, 0, 0))
        stiff = get(4, (0, 0, 0)) + 2.0 * mu
        shear_sides = []
        stiff_sides = []
        for d in range(3):
            for s in range(2):
                shift = moved(d, 1 - 2 * s)
                mu_side = get(3, shift)
                a = 0.5 * (mu + mu_side)
                b = 0.5 * (stiff + (get(4, shift) + 2.0 * mu_side))
                coef[d * 2 + s, level] = a
                coef[6 + d * 2 + s, level] = b
                shear_sides.append(a)
                stiff_sides.append(b)
        for i in range(3):
            total = None
            for d in range(3):
                sides = stiff_sides if d == i else shear_sides
                part = sides[2 * d] + sides[2 * d + 1]
                total = part if total is None else total + part
            coef[12 + i, level] = total
        dens_v[level] = step_square / dens_v[level]
        return carry

    def elastic(level, pads, index):
        cache = {}

        def get(c, shift):
            key = (c, shift)
            if key not in cache:
                dl, de, dn = shift
                cache[key] = pads[dn][index(c), level + 1 + dl, 8 + de:24 + de, :]
            return cache[key]

        kcache = {}

        def modulus(f, shift):
            key = (f, shift)
            if key not in kcache:
                dl, de, dn = shift
                kcache[key] = ku[dn][f, level + 1 + dl, 8 + de:24 + de, :]
            return kcache[key]

        def both(i, si, j, sj):
            a, b = moved(i, si), moved(j, sj)
            return tuple(p + q for p, q in zip(a, b))

        results = []
        for i in range(3):
            total = -coef[12 + i, level] * get(i, (0, 0, 0))
            for d in range(3):
                for s in range(2):
                    at = (6 if d == i else 0) + d * 2 + s
                    total = total + coef[at, level] * get(i, moved(d, 1 - 2 * s))
            mixed = None
            for j in range(3):
                if j == i:
                    continue
                pp = get(j, both(i, 1, j, 1))
                pm = get(j, both(i, 1, j, -1))
                mp = get(j, both(i, -1, j, 1))
                mm = get(j, both(i, -1, j, -1))
                part = (
                    modulus(4, moved(i, 1)) * (pp - pm)
                    - modulus(4, moved(i, -1)) * (mp - mm)
                    + modulus(3, moved(j, 1)) * (pp - mp)
                    - modulus(3, moved(j, -1)) * (pm - mm)
                )
                mixed = part if mixed is None else mixed + part
            results.append(total + 0.25 * mixed)
        return results

    copies_in[4].wait()
    lax.fori_loop(0, LEV, prepare, 0)
    copies_in[3].wait()

    def first_base(level, carry):
        applied = elastic(level, ku, lambda c: c)
        scale = dens_v[level]
        for c in range(3):
            now = ku0[c, level + 1, 8:24, :]
            base[c, level] = 2.0 * now - prev_v[c, level] + scale * applied[c]
        return carry

    lax.fori_loop(0, LEV, first_base, 0)

    slots_start(1)

    def incident(n):
        for copy in stage2[n]:
            copy.wait_recv()
        got = r2[n, 0]
        for y in range(1, NY):
            got = got + r2[n, y]
        eastern_a = dot_exact(east_a[...], got[0:32])
        eastern_b = dot_exact(east_b[...], got[32:48])
        for g in range(4):
            piece_a = eastern_a[g * 16:(g + 1) * 16]
            piece_b = eastern_b[g * 16:(g + 1) * 16]
            if g % 2:
                piece_b = pltpu.roll(piece_b, 64, 1)
            pieces = [piece_a, pltpu.roll(piece_a, 64, 1), piece_b]
            high, middle, _ = split(jnp.concatenate(pieces, axis=0))
            both = jnp.dot(
                jnp.concatenate([high, middle], axis=0), q_high[g], preferred_element_type=F32
            )
            rest = jnp.dot(high, q_low[g], preferred_element_type=F32)
            fine = both[:48] + (both[48:] + rest)
            for j in range(2):
                for c in range(3):
                    inc_v[n, c, 2 * g + j] = fine[c * 16:(c + 1) * 16, j * 128:(j + 1) * 128]
        phase = FORCE_0 + n
        flat = inc_v.reshape(6 * LEV * CE, CN)
        pack_rows(phase, flat, n * 3 * LEV * CE, LEV, CE, 3)
        halo_start(phase, range(6))
        zero = jnp.zeros((16, 128), F32)
        pack_cols(phase, lambda f, level: inc_v[n, f, level], 3, zero, zero)
        halo_start(phase, (6, 7))

    def mask_inside(n):
        def body(level, carry):
            outer = (low_level > level).astype(F32)
            inner = ((low_level <= level) & (high_level > level)).astype(F32)
            for c in range(3):
                cells = inc_v[n, c, level]
                values = (cells, pltpu.roll(cells, 1, 1), pltpu.roll(cells, 127, 1))
                for pad, value in zip((oi0, oim, oip), values):
                    pad[n * 6 + c, level + 1, 8:24, :] = outer * value
                    pad[n * 6 + 3 + c, level + 1, 8:24, :] = inner * value
            return carry

        for level in range(LEV):
            body(level, 0)

    def take_masked(n):
        phase = FORCE_0 + n
        halo_wait(phase)
        flats = [flat_of(p) for p in (oi0, oim, oip)]
        for c in range(3):
            for _, oi, row, m, lo, hi in take_rows(phase, c, 2):
                store_rows(flats, n * 6 + oi * 3 + c, row, (m, lo, hi))
        low, high = side_cols(phase)
        bounds = []
        for side in range(2):
            got = rcols[START, side]
            bounds.append([
                jnp.broadcast_to(got[:, 24 + b:25 + b], (16, 128)) for b in range(2)
            ])

        def body(level, carry):
            here = float(level)
            outer = [here < bounds[side][0] for side in range(2)]
            inner = [(here >= bounds[side][0]) & (here < bounds[side][1]) for side in range(2)]
            for c in range(3):
                place = c * 8 + level
                left = pltpu.roll(low, (128 - place) % 128, 1)
                right = pltpu.roll(high, 127 - place, 1)
                for oi, masks in ((0, outer), (1, inner)):
                    at = n * 6 + oi * 3 + c
                    at_m = oim[at, level + 1, 8:24, :]
                    at_p = oip[at, level + 1, 8:24, :]
                    new_m = jnp.where(masks[0], left, 0.0)
                    new_p = jnp.where(masks[1], right, 0.0)
                    oim[at, level + 1, 8:24, :] = jnp.where(lane16 == 0, new_m, at_m)
                    oip[at, level + 1, 8:24, :] = jnp.where(lane16 == 127, new_p, at_p)
            return carry

        for level in range(LEV):
            body(level, 0)

    incident(0)
    mask_inside(0)
    incident(1)

    oi = {-1: oim, 0: oi0, 1: oip}
    md = {-1: mdm, 0: md0, 1: mdp}

    def force(level, n):
        inside = (level >= low_level) & (level < high_level)
        which = n * 6 + jnp.where(inside, 0, 3)
        sign = inside.astype(F32) - (level < low_level).astype(F32)
        return sign, elastic(level, oi, lambda c: which + c)

    take_masked(0)

    def middle(level, carry):
        sign, applied = force(level, 0)
        scale = sign * dens_v[level]
        for c in range(3):
            cells = base[c, level] + scale * applied[c]
            md0[c, level + 1, 8:24, :] = cells
            mid_v[c, level] = cells
        return carry

    lax.fori_loop(0, LEV, middle, 0)
    pack_rows(MIDDLE, flat_of(md0), PITCH + 8, SLABS, PITCH, 3)
    halo_start(MIDDLE, range(6))
    zero = jnp.zeros((16, 128), F32)
    pack_cols(MIDDLE, padded_cells(md0, 0), 3, zero, zero)
    halo_start(MIDDLE, (6, 7))
    mask_inside(1)
    turn((md0, mdm, mdp), 0, 3)
    take_masked(1)

    def second_base(level, carry):
        sign, applied = force(level, 1)
        scale = sign * dens_v[level]
        for c in range(3):
            mid = md0[c, level + 1, 8:24, :]
            now = ku0[c, level + 1, 8:24, :]
            base[c, level] = 2.0 * mid - now + scale * applied[c]
        return carry

    lax.fori_loop(0, LEV, second_base, 0)
    for n in range(2):
        for copy in stage1[n] + stage2[n]:
            copy.wait_send()
    for phase in (START, FORCE_0, FORCE_1):
        halo_sent(phase)
    halo_wait(MIDDLE)
    take_edges(MIDDLE, (md0, mdm, mdp), 3)

    def last(level, carry):
        applied = elastic(level, md, lambda c: c)
        scale = dens_v[level]
        for c in range(3):
            nxt_v[c, level] = base[c, level] + scale * applied[c]
        return carry

    lax.fori_loop(0, LEV, last, 0)
    halo_sent(MIDDLE)


def hand_out(inc_v, mid_v, nxt_v, inc_h, mid_h, nxt_h, sems):
    copies = [
        pltpu.make_async_copy(src, dst, sems.at[i])
        for i, (src, dst) in enumerate(((inc_v, inc_h), (mid_v, mid_h), (nxt_v, nxt_h)))
    ]
    for copy in copies:
        copy.start()
    for copy in copies:
        copy.wait()


def local(disp_now, disp_prev, density, moduli, coarse, block_route, ranges, offsets):
    hbm = pl.BlockSpec(memory_space=pl.ANY)
    on_chip = pl.BlockSpec(memory_space=pltpu.VMEM)

    def vmem(*shape):
        return pltpu.VMEM(shape, F32)

    dma = pltpu.SemaphoreType.DMA
    outs = (
        jax.ShapeDtypeStruct((2, 3, LEV, CE, CN), F32),
        jax.ShapeDtypeStruct((3, LEV, CE, CN), F32),
        jax.ShapeDtypeStruct((3, LEV, CE, CN), F32),
    )
    args = (
        disp_now, disp_prev, density, moduli, coarse, block_route, ranges,
        offsets.transpose(0, 3, 1, 2),
    )
    results = pl.pallas_call(
        kernel,
        out_shape=outs,
        in_specs=[hbm] * 8,
        out_specs=(on_chip,) * 3,
        scratch_shapes=[
            pltpu.SMEM((256,), jnp.int32), pltpu.SMEM((1, 1, 2), jnp.int32),
            pltpu.SMEM((1, 3, 1, 4), jnp.int32),
            vmem(3, LEV, CE, CN), vmem(LEV, CE, CN), vmem(2, 24, 256), vmem(24, 256),
            vmem(192, 128), pltpu.SMEM((NY * 4,), jnp.int32),
            vmem(2, 3, 8, 128), vmem(NX * 3, 8, 128), vmem(NX * 3, 8, 128),
            vmem(2, NY, 48, 128), vmem(2, NY, 48, 128),
            pltpu.VMEM((64, 32), jnp.bfloat16), pltpu.VMEM((64, 16), jnp.bfloat16),
            pltpu.VMEM((4, 128, 256), jnp.bfloat16), pltpu.VMEM((4, 128, 256), jnp.bfloat16),
            *[vmem(5, SLABS, PITCH, CN)] * 3,
            *[vmem(12, SLABS, PITCH, CN)] * 3,
            *[vmem(3, SLABS, PITCH, CN)] * 3,
            vmem(15, LEV, CE, CN), vmem(3, LEV, CE, CN),
            vmem(4, 2, 48, 128), vmem(4, 2, 16, 128),
            vmem(4, 6, 48, 128), vmem(4, 2, 16, 128), vmem(6, 2, 8, 128),
            dma((4, 8)), dma((4, 8)), dma((2, NX)), dma((2, NX)), dma((2, NY)), dma((2, NY)),
            dma((8,)),
        ],
        compiler_params=pltpu.CompilerParams(
            collective_id=0, has_side_effects=True, vmem_limit_bytes=48 * 1024 * 1024
        ),
    )(*[pltpu.with_memory_space_constraint(v, pltpu.HBM) for v in args])
    return pl.pallas_call(
        hand_out,
        out_shape=outs,
        in_specs=[on_chip] * 3,
        out_specs=(hbm, hbm, hbm),
        scratch_shapes=[dma((3,))],
        compiler_params=pltpu.CompilerParams(vmem_limit_bytes=4 * 1024 * 1024),
    )(*results)


def solution(mesh):
    return jax.shard_map(
        local,
        mesh=mesh,
        in_specs=(
            P(None, None, "gx", "gy"),
            P(None, None, "gx", "gy"),
            P(None, "gx", "gy"),
            P(None, None, "gx", "gy"),
            P(("gx", "gy"), None, None),
            P(),
            P("gx", "gy", None),
            P("gx", "gy", None, None),
        ),
        out_specs=(
            P(None, None, None, "gx", "gy"),
            P(None, None, "gx", "gy"),
            P(None, None, "gx", "gy"),
        ),
        check_vma=False,
    )
```

```python
import jax
import jax.numpy as jnp
from jax import lax
from jax.experimental import pallas as pl
from jax.experimental.pallas import tpu as pltpu
from jax.sharding import PartitionSpec as P

step_square = 0.05
time_weights = ((-0.0595, 0.7735, 0.3315, -0.0455), (-0.063756, 0.607068, 0.517132, -0.060444))
NX, NY = 16, 8
LEV, CE, CN = 8, 16, 128
SLABS, PITCH = LEV + 2, 32
COARSE_EAST, COARSE_NORTH = 8, 26
MESH = pl.DeviceIdType.MESH
FAR_X = (10, 9, 11, 6, 14, 7, 5, 13, 15, 8, 2, 4, 12, 1, 3)
FAR_Y = (4, 3, 5, 2, 6, 1, 7)
F32 = jnp.float32
START, FORCE_0, FORCE_1, MIDDLE = range(4)


def iota(shape, dim):
    return lax.broadcasted_iota(jnp.int32, shape, dim)


def split(x):
    high = x.astype(jnp.bfloat16)
    rest = x - high.astype(F32)
    middle = rest.astype(jnp.bfloat16)
    low = (rest - middle.astype(F32)).astype(jnp.bfloat16)
    return high, middle, low


def dot_exact(whole, x):
    parts = [jnp.dot(whole, part, preferred_element_type=F32) for part in split(x)]
    return (parts[2] + parts[1]) + parts[0]


def kernel(
    now_h, prev_h, dens_h, mod_h, coarse_h, route_h, ranges_h, offs_h,
    inc_v, mid_v, nxt_v,
    route_s, ranges_s, offs_s, prev_v, dens_v, coarse_v, timed_v, turned_v,
    found_s, pay_v, r1_0, r1_1, out2, r2, east_a, east_b, q_high, q_low,
    ku0, kum, kup, oi0, oim, oip, md0, mdm, mdp,
    coef, base, srows, scols, rrows, rcols, row_masks,
    hsend, hrecv, send1, recv1, send2, recv2, local_sem,
):
    gx = lax.axis_index("gx")
    gy = lax.axis_index("gy")

    def x_at(d):
        return lax.rem(gx + (d + NX), NX)

    def y_at(d):
        return lax.rem(gy + (d + NY), NY)

    has_x = {1: gx < NX - 1, -1: gx > 0, 0: None}
    has_y = {1: gy < NY - 1, -1: gy > 0, 0: None}

    def has(a, b):
        if a and b:
            return has_x[a] & has_y[b]
        return has_x[a] if a else has_y[b]

    copies_in = [
        pltpu.make_async_copy(coarse_h, coarse_v, local_sem.at[0]),
        pltpu.make_async_copy(mod_h, ku0.at[3:5, 1:9, 8:24, :], local_sem.at[1]),
        pltpu.make_async_copy(now_h, ku0.at[0:3, 1:9, 8:24, :], local_sem.at[2]),
        pltpu.make_async_copy(prev_h, prev_v, local_sem.at[3]),
        pltpu.make_async_copy(dens_h, dens_v, local_sem.at[4]),
        pltpu.make_async_copy(route_h, route_s, local_sem.at[5]),
        pltpu.make_async_copy(ranges_h, ranges_s, local_sem.at[6]),
        pltpu.make_async_copy(offs_h, offs_s, local_sem.at[7]),
    ]
    for at in (0, 1, 2):
        copies_in[at].start()

    barrier = pltpu.get_barrier_semaphore()
    for d in range(1, NX):
        pl.semaphore_signal(barrier, inc=1, device_id=(x_at(d), gy), device_id_type=MESH)
    for d in range(1, NY):
        pl.semaphore_signal(barrier, inc=1, device_id=(gx, y_at(d)), device_id_type=MESH)
    for a in (-1, 1):
        for b in (-1, 1):

            @pl.when(has(a, b))
            def _(a=a, b=b):
                pl.semaphore_signal(
                    barrier, inc=1, device_id=(gx + a, gy + b), device_id_type=MESH
                )

    for at in (5, 6, 7, 3, 4):
        copies_in[at].start()

    lane8 = iota((8, 128), 1)
    sub8 = iota((8, 128), 0)
    lane16 = iota((16, 128), 1)

    copies_in[0].wait()
    for n in range(2):
        for k in range(2):
            row = (n * 2 + k) * 6
            total = None
            for t in range(4):
                term = time_weights[n][t] * coarse_v[k, t * 6:t * 6 + 6, :]
                total = term if total is None else total + term
            timed_v[row:row + 6, :] = total
    timed = timed_v[...]
    for a in range(COARSE_EAST):
        shifted = timed if a == 0 else pltpu.roll(timed, 256 - COARSE_NORTH * a, 1)
        turned_v[a * 24:(a + 1) * 24, :] = shifted[:, :128]
    for n in range(2):
        places = [[(n * 2 + k) * 6 + p for p in range(4)] for k in range(2)]
        places.append([(n * 2 + k) * 6 + p for k in range(2) for p in (4, 5)])
        for at, rows in enumerate(places):
            joined = None
            for part, row in enumerate(rows):
                piece = turned_v[pl.ds(row, 8, stride=24), :]
                if part:
                    piece = pltpu.roll(piece, part * 32, 1)
                here = (lane8 >= part * 32) & (lane8 < part * 32 + COARSE_NORTH)
                joined = jnp.where(here, piece, 0.0 if joined is None else joined)
            pay_v[n, at] = joined

    WAYS = ((1, 1), (1, -1), (-1, 1), (-1, -1), (1, 0), (-1, 0), (0, 1), (0, -1))

    def slot_of(f):
        return f if f < 3 else f + 1

    def halo_copies(phase):
        plan = []
        for i, (a, b) in enumerate(WAYS):
            rows = 24
            if phase == START:
                rows = 32 if b else 48
            if a:
                src = srows.at[phase, 0 if a > 0 else 1, :rows]
                dst = rrows.at[phase, i, :rows]
            else:
                src = scols.at[phase, i - 6]
                dst = rcols.at[phase, i - 6]
            plan.append(
                pltpu.make_async_remote_copy(
                    src, dst, hsend.at[phase], hrecv.at[phase],
                    device_id=(gx + a, gy + b), device_id_type=MESH,
                )
            )
        return plan

    halos = [halo_copies(phase) for phase in range(4)]

    def halo_start(phase, which):
        for i in which:

            @pl.when(has(*WAYS[i]))
            def _(i=i):
                halos[phase][i].start()

    count_x = has_x[1].astype(jnp.int32) + has_x[-1].astype(jnp.int32)
    count_y = has_y[1].astype(jnp.int32) + has_y[-1].astype(jnp.int32)

    def all_of(ref, sem):
        return pltpu.make_async_copy(ref, ref, sem)

    def halo_all(phase, sem):
        side, corner = (48, 32) if phase == START else (24, 24)
        flat = rrows.reshape(4 * 6 * 48, CN)
        for nx in (1, 2):
            for ny in (1, 2):
                rows = nx * side + nx * ny * corner + ny * 16

                @pl.when((count_x == nx) & (count_y == ny))
                def _(rows=rows):
                    all_of(flat.at[pl.ds(phase * 6 * 48, rows)], sem.at[phase]).wait()

    def halo_wait(phase):
        halo_all(phase, hrecv)

    def halo_sent(phase):
        halo_all(phase, hsend)

    def pack_rows(phase, flat, first, slab, pitch, fields):
        for f in range(fields):
            start = first + f * slab * pitch
            at = slot_of(f) * 8
            srows[phase, 0, at:at + 8, :] = flat[pl.ds(start + CE - 1, 8, stride=pitch), :]
            srows[phase, 1, at:at + 8, :] = flat[pl.ds(start, 8, stride=pitch), :]

    def pack_cols(phase, cells_at, fields, high, low):
        def pack(level, carry):
            high, low = carry
            for f in range(fields):
                cells = cells_at(f, level)
                place = slot_of(f) * 8 + level
                here = lane16 == place
                high = jnp.where(here, pltpu.roll(cells, place + 1, 1), high)
                low = jnp.where(here, pltpu.roll(cells, place, 1), low)
            return high, low

        for level in range(LEV):
            high, low = pack(level, (high, low))
        scols[phase, 0] = high
        scols[phase, 1] = low

    def flat_of(pad):
        return pad.reshape(pad.shape[0] * SLABS * PITCH, CN)

    def padded_cells(pad, first):
        return lambda f, level: pad[first + f, level + 1, 8:24, :]

    SIDES = ((4, 0, 1, -1, 7), (5, 2, 3, 1, 24))

    def take_rows(phase, f, masks):
        out = []
        for side, (own, left, right, a, row) in enumerate(SIDES):
            here = slice(slot_of(f) * 8, slot_of(f) * 8 + 8)
            middle = jnp.where(has(a, 0), rrows[phase, own, here, :], 0.0)
            minus = plus = jnp.zeros((8, 128), F32)
            if f < 3:
                minus = jnp.where(has(a, -1), rrows[phase, left, here, :], 0.0)
                plus = jnp.where(has(a, 1), rrows[phase, right, here, :], 0.0)
            for oi in range(masks):
                m, lo, hi = middle, minus, plus
                if masks > 1:
                    m = m * row_masks[own, oi]
                    lo = lo * row_masks[left, oi]
                    hi = hi * row_masks[right, oi]
                out.append((
                    side, oi, row, m,
                    pltpu.roll(jnp.where(lane8 == 127, lo, m), 1, 1),
                    pltpu.roll(jnp.where(lane8 == 0, hi, m), 127, 1),
                ))
        return out

    def store_rows(flats, index, row, values):
        where = pl.ds((index * SLABS + 1) * PITCH + row, 8, stride=PITCH)
        for flat, value in zip(flats, values):
            flat[where, :] = value

    def side_cols(phase):
        low = jnp.where(has(0, -1), rcols[phase, 0], 0.0)
        high = jnp.where(has(0, 1), rcols[phase, 1], 0.0)
        return low, high

    def turn(pads, first, fields):
        pad, pad_m, pad_p = pads

        def body(level, carry):
            for f in range(fields):
                cells = pad[first + f, level + 1, 8:24, :]
                pad_m[first + f, level + 1, 8:24, :] = pltpu.roll(cells, 1, 1)
                pad_p[first + f, level + 1, 8:24, :] = pltpu.roll(cells, 127, 1)
            return carry

        for level in range(LEV):
            body(level, 0)

    def take_edges(phase, pads, fields):
        _, pad_m, pad_p = pads
        flats = [flat_of(p) for p in pads]
        for f in range(fields):
            for _, _, row, m, lo, hi in take_rows(phase, f, 1):
                store_rows(flats, f, row, (m, lo, hi))
        low, high = side_cols(phase)

        def body(level, carry):
            for f in range(fields):
                place = slot_of(f) * 8 + level
                left = pltpu.roll(low, (128 - place) % 128, 1)
                right = pltpu.roll(high, 127 - place, 1)
                at_m = pad_m[f, level + 1, 8:24, :]
                at_p = pad_p[f, level + 1, 8:24, :]
                pad_m[f, level + 1, 8:24, :] = jnp.where(lane16 == 0, left, at_m)
                pad_p[f, level + 1, 8:24, :] = jnp.where(lane16 == 127, right, at_p)
            return carry

        for level in range(LEV):
            body(level, 0)

    pl.semaphore_wait(barrier, NX - 1 + NY - 1 + count_x * count_y)

    r1 = (r1_0, r1_1)

    stage1 = [
        [
            pltpu.make_async_remote_copy(
                pay_v.at[n], r1[n].at[pl.ds(gx * 3, 3)], send1.at[n], recv1.at[n],
                device_id=(x_at(d), gy), device_id_type=MESH,
            )
            for d in FAR_X
        ]
        for n in range(2)
    ]
    stage2 = [[], []]

    def line_start(n):
        for copy in stage1[n]:
            copy.start()
        r1[n][pl.ds(gx * 3, 3)] = pay_v[n]

    lane_half = lane8 < 64

    def slots_start(n):
        all_of(r1[n].at[0:3 * (NX - 1)], recv1.at[n]).wait()

        def fill(to, carry):
            halves = []
            for g in range(4):
                place = found_s[to * 4 + g]
                at = jnp.clip(place - 1, 0, 3 * NX - 2)
                k = lax.rem(at, 3)
                first = r1[n][at]
                second = r1[n][at - k + 2]
                second = pltpu.roll(second, 64 * lax.rem(k + g, 2), 1)
                out2[n, to, g * 8:(g + 1) * 8, :] = jnp.where(place > 0, first, 0.0)
                halves.append(jnp.where(place > 0, second, 0.0))
            for h in range(2):
                joined = jnp.where(lane_half, halves[2 * h], halves[2 * h + 1])
                out2[n, to, 32 + h * 8:40 + h * 8, :] = joined
            return carry

        for d in FAR_Y + (0,):
            to = y_at(d)
            fill(to, 0)
            if d == 0:
                continue
            copy = pltpu.make_async_remote_copy(
                out2.at[n, to], r2.at[n, gy], send2.at[n], recv2.at[n],
                device_id=(gx, to), device_id_type=MESH,
            )
            copy.start()
            stage2[n].append(copy)
        r2[n, gy] = out2[n, gy]

    line_start(0)
    for copy in copies_in[5:]:
        copy.wait()
    low_level = ranges_s[0, 0, 0]
    high_level = ranges_s[0, 0, 1]
    copies_in[1].wait()
    copies_in[2].wait()
    range_rows = jnp.where(sub8 == 0, low_level, high_level).astype(F32)
    pack_rows(START, flat_of(ku0), PITCH + 8, SLABS, PITCH, 5)
    for side in range(2):
        srows[START, side, 24:32, :] = range_rows
    range_cols = jnp.where(lane16 == 24, low_level, high_level).astype(F32)
    pack_cols(START, padded_cells(ku0, 0), 5, range_cols, range_cols)
    turn((ku0, kum, kup), 0, 5)

    halo_start(START, range(8))
    line_start(1)
    blank = jnp.zeros((PITCH, CN), F32)
    for pads, fields in (((ku0, kum, kup), 5), ((oi0, oim, oip), 12), ((md0, mdm, mdp), 3)):

        def clear(f, carry, pads=pads):
            for pad in pads:
                pad[f, 0] = blank
                pad[f, SLABS - 1] = blank
            return carry

        lax.fori_loop(0, fields, clear, 0)

    def find(slot, carry):
        place = jnp.int32(0)
        for x in range(NX):
            for k in range(2):
                named = route_s[(x * NY + gy) * 2 + k] == gx * 32 + slot
                place = jnp.maximum(place, jnp.where(named, 1 + 3 * x + k, 0))
        found_s[slot] = place
        return carry

    lax.fori_loop(0, NY * 4, find, 0)

    def hat25(cells, points):
        return jnp.maximum(25 - jnp.abs(4 * cells - 25 * points), 0).astype(F32)

    for g in range(4):
        for ref, count in ((east_a, 4), (east_b, 2)):
            shape = (16, count * 8)
            cells = iota(shape, 0) + offs_s[0, 1, 0, g]
            cols = iota(shape, 1)
            weights = hat25(cells, lax.rem(cols, 8))
            mine = lax.div(cols, 8) == (g if count == 4 else g // 2)
            ref[g * 16:(g + 1) * 16, :] = jnp.where(mine, weights, 0.0).astype(jnp.bfloat16)
        point = iota((128, 256), 0)
        cell = iota((128, 256), 1)
        north = hat25(lax.rem(cell, 128) + offs_s[0, 2, 0, g], lax.rem(point, 32)) * (1.0 / 625.0)
        depth = (offs_s[0, 0, 0, g] + lax.div(cell, 128)).astype(F32) * (4.0 / 25.0)
        upright = jnp.where(point < 32, 1.0 - depth, depth)
        keep = (point < 64) & (lax.rem(point, 32) < COARSE_NORTH)
        weights = jnp.where(keep, north * upright, 0.0)
        high = weights.astype(jnp.bfloat16)
        q_high[g] = high
        q_low[g] = (weights - high.astype(F32)).astype(jnp.bfloat16)

    slots_start(0)

    halo_wait(START)
    take_edges(START, (ku0, kum, kup), 5)
    level8 = sub8.astype(F32)
    for i in range(6):
        low = rrows[START, i, 24:25, :]
        high = rrows[START, i, 25:26, :]
        row_masks[i, 0] = jnp.where(level8 < low, 1.0, 0.0)
        row_masks[i, 1] = jnp.where((level8 >= low) & (level8 < high), 1.0, 0.0)
    ku = {-1: kum, 0: ku0, 1: kup}
    steps = ((1, 0, 0), (0, 1, 0), (0, 0, 1))

    def moved(d, sign):
        return tuple(sign * s for s in steps[d])

    def prepare(level, carry):
        def get(f, shift):
            dl, de, dn = shift
            return ku[dn][f, level + 1 + dl, 8 + de:24 + de, :]

        mu = get(3, (0, 0, 0))
        stiff = get(4, (0, 0, 0)) + 2.0 * mu
        shear_sides = []
        stiff_sides = []
        for d in range(3):
            for s in range(2):
                shift = moved(d, 1 - 2 * s)
                mu_side = get(3, shift)
                a = 0.5 * (mu + mu_side)
                b = 0.5 * (stiff + (get(4, shift) + 2.0 * mu_side))
                coef[d * 2 + s, level] = a
                coef[6 + d * 2 + s, level] = b
                shear_sides.append(a)
                stiff_sides.append(b)
        for i in range(3):
            total = None
            for d in range(3):
                sides = stiff_sides if d == i else shear_sides
                part = sides[2 * d] + sides[2 * d + 1]
                total = part if total is None else total + part
            coef[12 + i, level] = total
        dens_v[level] = step_square / dens_v[level]
        return carry

    def elastic(level, pads, index):
        cache = {}

        def get(c, shift):
            key = (c, shift)
            if key not in cache:
                dl, de, dn = shift
                cache[key] = pads[dn][index(c), level + 1 + dl, 8 + de:24 + de, :]
            return cache[key]

        kcache = {}

        def modulus(f, shift):
            key = (f, shift)
            if key not in kcache:
                dl, de, dn = shift
                kcache[key] = ku[dn][f, level + 1 + dl, 8 + de:24 + de, :]
            return kcache[key]

        def both(i, si, j, sj):
            a, b = moved(i, si), moved(j, sj)
            return tuple(p + q for p, q in zip(a, b))

        results = []
        for i in range(3):
            total = -coef[12 + i, level] * get(i, (0, 0, 0))
            for d in range(3):
                for s in range(2):
                    at = (6 if d == i else 0) + d * 2 + s
                    total = total + coef[at, level] * get(i, moved(d, 1 - 2 * s))
            mixed = None
            for j in range(3):
                if j == i:
                    continue
                pp = get(j, both(i, 1, j, 1))
                pm = get(j, both(i, 1, j, -1))
                mp = get(j, both(i, -1, j, 1))
                mm = get(j, both(i, -1, j, -1))
                part = (
                    modulus(4, moved(i, 1)) * (pp - pm)
                    - modulus(4, moved(i, -1)) * (mp - mm)
                    + modulus(3, moved(j, 1)) * (pp - mp)
                    - modulus(3, moved(j, -1)) * (pm - mm)
                )
                mixed = part if mixed is None else mixed + part
            results.append(total + 0.25 * mixed)
        return results

    copies_in[4].wait()
    lax.fori_loop(0, LEV, prepare, 0)
    copies_in[3].wait()

    def first_base(level, carry):
        applied = elastic(level, ku, lambda c: c)
        scale = dens_v[level]
        for c in range(3):
            now = ku0[c, level + 1, 8:24, :]
            base[c, level] = 2.0 * now - prev_v[c, level] + scale * applied[c]
        return carry

    lax.fori_loop(0, LEV, first_base, 0)

    slots_start(1)

    def incident(n):
        all_of(r2.at[n, 0:NY - 1], recv2.at[n]).wait()
        got = r2[n, 0]
        for y in range(1, NY):
            got = got + r2[n, y]
        eastern_a = dot_exact(east_a[...], got[0:32])
        eastern_b = dot_exact(east_b[...], got[32:48])
        for g in range(4):
            piece_a = eastern_a[g * 16:(g + 1) * 16]
            piece_b = eastern_b[g * 16:(g + 1) * 16]
            if g % 2:
                piece_b = pltpu.roll(piece_b, 64, 1)
            pieces = [piece_a, pltpu.roll(piece_a, 64, 1), piece_b]
            high, middle, _ = split(jnp.concatenate(pieces, axis=0))
            both = jnp.dot(
                jnp.concatenate([high, middle], axis=0), q_high[g], preferred_element_type=F32
            )
            rest = jnp.dot(high, q_low[g], preferred_element_type=F32)
            fine = both[:48] + (both[48:] + rest)
            for j in range(2):
                for c in range(3):
                    inc_v[n, c, 2 * g + j] = fine[c * 16:(c + 1) * 16, j * 128:(j + 1) * 128]
        phase = FORCE_0 + n
        flat = inc_v.reshape(6 * LEV * CE, CN)
        pack_rows(phase, flat, n * 3 * LEV * CE, LEV, CE, 3)
        halo_start(phase, range(6))
        zero = jnp.zeros((16, 128), F32)
        pack_cols(phase, lambda f, level: inc_v[n, f, level], 3, zero, zero)
        halo_start(phase, (6, 7))

    def mask_inside(n):
        def body(level, carry):
            outer = (low_level > level).astype(F32)
            inner = ((low_level <= level) & (high_level > level)).astype(F32)
            for c in range(3):
                cells = inc_v[n, c, level]
                values = (cells, pltpu.roll(cells, 1, 1), pltpu.roll(cells, 127, 1))
                for pad, value in zip((oi0, oim, oip), values):
                    pad[n * 6 + c, level + 1, 8:24, :] = outer * value
                    pad[n * 6 + 3 + c, level + 1, 8:24, :] = inner * value
            return carry

        for level in range(LEV):
            body(level, 0)

    def take_masked(n):
        phase = FORCE_0 + n
        halo_wait(phase)
        flats = [flat_of(p) for p in (oi0, oim, oip)]
        for c in range(3):
            for _, oi, row, m, lo, hi in take_rows(phase, c, 2):
                store_rows(flats, n * 6 + oi * 3 + c, row, (m, lo, hi))
        low, high = side_cols(phase)
        bounds = []
        for side in range(2):
            got = rcols[START, side]
            bounds.append([
                jnp.broadcast_to(got[:, 24 + b:25 + b], (16, 128)) for b in range(2)
            ])

        def body(level, carry):
            here = float(level)
            outer = [here < bounds[side][0] for side in range(2)]
            inner = [(here >= bounds[side][0]) & (here < bounds[side][1]) for side in range(2)]
            for c in range(3):
                place = c * 8 + level
                left = pltpu.roll(low, (128 - place) % 128, 1)
                right = pltpu.roll(high, 127 - place, 1)
                for oi, masks in ((0, outer), (1, inner)):
                    at = n * 6 + oi * 3 + c
                    at_m = oim[at, level + 1, 8:24, :]
                    at_p = oip[at, level + 1, 8:24, :]
                    new_m = jnp.where(masks[0], left, 0.0)
                    new_p = jnp.where(masks[1], right, 0.0)
                    oim[at, level + 1, 8:24, :] = jnp.where(lane16 == 0, new_m, at_m)
                    oip[at, level + 1, 8:24, :] = jnp.where(lane16 == 127, new_p, at_p)
            return carry

        for level in range(LEV):
            body(level, 0)

    incident(0)
    mask_inside(0)
    incident(1)

    oi = {-1: oim, 0: oi0, 1: oip}
    md = {-1: mdm, 0: md0, 1: mdp}

    def force(level, n):
        inside = (level >= low_level) & (level < high_level)
        which = n * 6 + jnp.where(inside, 0, 3)
        sign = inside.astype(F32) - (level < low_level).astype(F32)
        return sign, elastic(level, oi, lambda c: which + c)

    take_masked(0)

    def middle(level, carry):
        sign, applied = force(level, 0)
        scale = sign * dens_v[level]
        for c in range(3):
            cells = base[c, level] + scale * applied[c]
            md0[c, level + 1, 8:24, :] = cells
            mid_v[c, level] = cells
        return carry

    lax.fori_loop(0, LEV, middle, 0)
    pack_rows(MIDDLE, flat_of(md0), PITCH + 8, SLABS, PITCH, 3)
    halo_start(MIDDLE, range(6))
    zero = jnp.zeros((16, 128), F32)
    pack_cols(MIDDLE, padded_cells(md0, 0), 3, zero, zero)
    halo_start(MIDDLE, (6, 7))
    mask_inside(1)
    turn((md0, mdm, mdp), 0, 3)
    take_masked(1)

    def second_base(level, carry):
        sign, applied = force(level, 1)
        scale = sign * dens_v[level]
        for c in range(3):
            mid = md0[c, level + 1, 8:24, :]
            now = ku0[c, level + 1, 8:24, :]
            base[c, level] = 2.0 * mid - now + scale * applied[c]
        return carry

    lax.fori_loop(0, LEV, second_base, 0)
    for n in range(2):
        all_of(r1[n].at[0:3 * (NX - 1)], send1.at[n]).wait()
        all_of(r2.at[n, 0:NY - 1], send2.at[n]).wait()
    for phase in (START, FORCE_0, FORCE_1):
        halo_sent(phase)
    halo_wait(MIDDLE)
    take_edges(MIDDLE, (md0, mdm, mdp), 3)

    def last(level, carry):
        applied = elastic(level, md, lambda c: c)
        scale = dens_v[level]
        for c in range(3):
            nxt_v[c, level] = base[c, level] + scale * applied[c]
        return carry

    lax.fori_loop(0, LEV, last, 0)
    halo_sent(MIDDLE)


def hand_out(inc_v, mid_v, nxt_v, inc_h, mid_h, nxt_h, sems):
    copies = [
        pltpu.make_async_copy(src, dst, sems.at[i])
        for i, (src, dst) in enumerate(((inc_v, inc_h), (mid_v, mid_h), (nxt_v, nxt_h)))
    ]
    for copy in copies:
        copy.start()
    for copy in copies:
        copy.wait()


def local(disp_now, disp_prev, density, moduli, coarse, block_route, ranges, offsets):
    hbm = pl.BlockSpec(memory_space=pl.ANY)
    on_chip = pl.BlockSpec(memory_space=pltpu.VMEM)

    def vmem(*shape):
        return pltpu.VMEM(shape, F32)

    dma = pltpu.SemaphoreType.DMA
    outs = (
        jax.ShapeDtypeStruct((2, 3, LEV, CE, CN), F32),
        jax.ShapeDtypeStruct((3, LEV, CE, CN), F32),
        jax.ShapeDtypeStruct((3, LEV, CE, CN), F32),
    )
    args = (
        disp_now, disp_prev, density, moduli, coarse, block_route, ranges,
        offsets.transpose(0, 3, 1, 2),
    )
    results = pl.pallas_call(
        kernel,
        out_shape=outs,
        in_specs=[hbm] * 8,
        out_specs=(on_chip,) * 3,
        scratch_shapes=[
            pltpu.SMEM((256,), jnp.int32), pltpu.SMEM((1, 1, 2), jnp.int32),
            pltpu.SMEM((1, 3, 1, 4), jnp.int32),
            vmem(3, LEV, CE, CN), vmem(LEV, CE, CN), vmem(2, 24, 256), vmem(24, 256),
            vmem(192, 128), pltpu.SMEM((NY * 4,), jnp.int32),
            vmem(2, 3, 8, 128), vmem(NX * 3, 8, 128), vmem(NX * 3, 8, 128),
            vmem(2, NY, 48, 128), vmem(2, NY, 48, 128),
            pltpu.VMEM((64, 32), jnp.bfloat16), pltpu.VMEM((64, 16), jnp.bfloat16),
            pltpu.VMEM((4, 128, 256), jnp.bfloat16), pltpu.VMEM((4, 128, 256), jnp.bfloat16),
            *[vmem(5, SLABS, PITCH, CN)] * 3,
            *[vmem(12, SLABS, PITCH, CN)] * 3,
            *[vmem(3, SLABS, PITCH, CN)] * 3,
            vmem(15, LEV, CE, CN), vmem(3, LEV, CE, CN),
            vmem(4, 2, 48, 128), vmem(4, 2, 16, 128),
            vmem(4, 6, 48, 128), vmem(4, 2, 16, 128), vmem(6, 2, 8, 128),
            dma((4,)), dma((4,)), dma((2,)), dma((2,)), dma((2,)), dma((2,)),
            dma((8,)),
        ],
        compiler_params=pltpu.CompilerParams(
            collective_id=0, has_side_effects=True, vmem_limit_bytes=48 * 1024 * 1024
        ),
    )(*[pltpu.with_memory_space_constraint(v, pltpu.HBM) for v in args])
    return pl.pallas_call(
        hand_out,
        out_shape=outs,
        in_specs=[on_chip] * 3,
        out_specs=(hbm, hbm, hbm),
        scratch_shapes=[dma((3,))],
        compiler_params=pltpu.CompilerParams(vmem_limit_bytes=4 * 1024 * 1024),
    )(*results)


def solution(mesh):
    return jax.shard_map(
        local,
        mesh=mesh,
        in_specs=(
            P(None, None, "gx", "gy"),
            P(None, None, "gx", "gy"),
            P(None, "gx", "gy"),
            P(None, None, "gx", "gy"),
            P(("gx", "gy"), None, None),
            P(),
            P("gx", "gy", None),
            P("gx", "gy", None, None),
        ),
        out_specs=(
            P(None, None, None, "gx", "gy"),
            P(None, None, "gx", "gy"),
            P(None, None, "gx", "gy"),
        ),
        check_vma=False,
    )
```

```python
import jax
import jax.numpy as jnp
from jax import lax
from jax.experimental import pallas as pl
from jax.experimental.pallas import tpu as pltpu
from jax.sharding import PartitionSpec as P

step_square = 0.05
time_weights = ((-0.0595, 0.7735, 0.3315, -0.0455), (-0.063756, 0.607068, 0.517132, -0.060444))
NX, NY = 16, 8
LEV, CE, CN = 8, 16, 128
SLABS, PITCH = LEV + 2, 32
COARSE_EAST, COARSE_NORTH = 8, 26
MESH = pl.DeviceIdType.MESH
PARTS = 4
FAR_X = (10, 9, 11, 6, 14, 7, 5, 13, 15, 8, 2, 4, 12, 1, 3)
FAR_Y = (4, 3, 5, 2, 6, 1, 7)
F32 = jnp.float32
START, FORCE_0, FORCE_1, MIDDLE = range(4)


def iota(shape, dim):
    return lax.broadcasted_iota(jnp.int32, shape, dim)


def split(x):
    high = x.astype(jnp.bfloat16)
    rest = x - high.astype(F32)
    middle = rest.astype(jnp.bfloat16)
    low = (rest - middle.astype(F32)).astype(jnp.bfloat16)
    return high, middle, low


def dot_exact(whole, x):
    parts = [jnp.dot(whole, part, preferred_element_type=F32) for part in split(x)]
    return (parts[2] + parts[1]) + parts[0]


steps = ((1, 0, 0), (0, 1, 0), (0, 0, 1))


def moved(d, sign):
    return tuple(sign * s for s in steps[d])


def elastic_at(level, pads, index, ku, coef):
    cache = {}

    def get(c, shift):
        key = (c, shift)
        if key not in cache:
            dl, de, dn = shift
            cache[key] = pads[dn][index(c), level + 1 + dl, 8 + de:24 + de, :]
        return cache[key]

    kcache = {}

    def modulus(f, shift):
        key = (f, shift)
        if key not in kcache:
            dl, de, dn = shift
            kcache[key] = ku[dn][f, level + 1 + dl, 8 + de:24 + de, :]
        return kcache[key]

    def both(i, si, j, sj):
        a, b = moved(i, si), moved(j, sj)
        return tuple(p + q for p, q in zip(a, b))

    results = []
    for i in range(3):
        total = -coef[12 + i, level] * get(i, (0, 0, 0))
        for d in range(3):
            for s in range(2):
                at = (6 if d == i else 0) + d * 2 + s
                total = total + coef[at, level] * get(i, moved(d, 1 - 2 * s))
        mixed = None
        for j in range(3):
            if j == i:
                continue
            pp = get(j, both(i, 1, j, 1))
            pm = get(j, both(i, 1, j, -1))
            mp = get(j, both(i, -1, j, 1))
            mm = get(j, both(i, -1, j, -1))
            part = (
                modulus(4, moved(i, 1)) * (pp - pm)
                - modulus(4, moved(i, -1)) * (mp - mm)
                + modulus(3, moved(j, 1)) * (pp - mp)
                - modulus(3, moved(j, -1)) * (pm - mm)
            )
            mixed = part if mixed is None else mixed + part
        results.append(total + 0.25 * mixed)
    return results


def kernel(
    now_h, prev_h, dens_h, mod_h, coarse_h, route_h, ranges_h, offs_h,
    inc_v, mid_v, ku0, kum, kup, md0, mdm, mdp, coef, base, dens_v,
    route_s, ranges_s, offs_s, prev_v, coarse_v, timed_v, turned_v,
    found_s, pay_v, r1_0, r1_1, out2, r2, east_a, east_b, q_high, q_low,
    oi0, oim, oip, srows, scols, rrows, rcols, row_masks,
    hsend, hrecv, send1, recv1, send2, recv2, local_sem,
):
    gx = lax.axis_index("gx")
    gy = lax.axis_index("gy")

    def x_at(d):
        return lax.rem(gx + (d + NX), NX)

    def y_at(d):
        return lax.rem(gy + (d + NY), NY)

    has_x = {1: gx < NX - 1, -1: gx > 0, 0: None}
    has_y = {1: gy < NY - 1, -1: gy > 0, 0: None}

    def has(a, b):
        if a and b:
            return has_x[a] & has_y[b]
        return has_x[a] if a else has_y[b]

    copies_in = [
        pltpu.make_async_copy(coarse_h, coarse_v, local_sem.at[0]),
        pltpu.make_async_copy(mod_h, ku0.at[3:5, 1:9, 8:24, :], local_sem.at[1]),
        pltpu.make_async_copy(now_h, ku0.at[0:3, 1:9, 8:24, :], local_sem.at[2]),
        pltpu.make_async_copy(prev_h, prev_v, local_sem.at[3]),
        pltpu.make_async_copy(dens_h, dens_v, local_sem.at[4]),
        pltpu.make_async_copy(route_h, route_s, local_sem.at[5]),
        pltpu.make_async_copy(ranges_h, ranges_s, local_sem.at[6]),
        pltpu.make_async_copy(offs_h, offs_s, local_sem.at[7]),
    ]
    for at in (0, 1, 2):
        copies_in[at].start()

    barrier = pltpu.get_barrier_semaphore()
    for d in range(1, NX):
        pl.semaphore_signal(barrier, inc=1, device_id=(x_at(d), gy), device_id_type=MESH)
    for d in range(1, NY):
        pl.semaphore_signal(barrier, inc=1, device_id=(gx, y_at(d)), device_id_type=MESH)
    for a in (-1, 1):
        for b in (-1, 1):

            @pl.when(has(a, b))
            def _(a=a, b=b):
                pl.semaphore_signal(
                    barrier, inc=1, device_id=(gx + a, gy + b), device_id_type=MESH
                )

    for at in (5, 6, 7, 3, 4):
        copies_in[at].start()

    lane8 = iota((8, 128), 1)
    sub8 = iota((8, 128), 0)
    lane16 = iota((16, 128), 1)

    copies_in[0].wait()
    for n in range(2):
        for k in range(2):
            row = (n * 2 + k) * 6
            total = None
            for t in range(4):
                term = time_weights[n][t] * coarse_v[k, t * 6:t * 6 + 6, :]
                total = term if total is None else total + term
            timed_v[row:row + 6, :] = total
    timed = timed_v[...]
    for a in range(COARSE_EAST):
        shifted = timed if a == 0 else pltpu.roll(timed, 256 - COARSE_NORTH * a, 1)
        turned_v[a * 24:(a + 1) * 24, :] = shifted[:, :128]
    for n in range(2):
        places = [[(n * 2 + k) * 6 + p for p in range(4)] for k in range(2)]
        places.append([(n * 2 + k) * 6 + p for k in range(2) for p in (4, 5)])
        for at, rows in enumerate(places):
            joined = None
            for part, row in enumerate(rows):
                piece = turned_v[pl.ds(row, 8, stride=24), :]
                if part:
                    piece = pltpu.roll(piece, part * 32, 1)
                here = (lane8 >= part * 32) & (lane8 < part * 32 + COARSE_NORTH)
                joined = jnp.where(here, piece, 0.0 if joined is None else joined)
            pay_v[n, at] = joined

    WAYS = ((1, 1), (1, -1), (-1, 1), (-1, -1), (1, 0), (-1, 0), (0, 1), (0, -1))

    def slot_of(f):
        return f if f < 3 else f + 1

    def halo_copies(phase):
        plan = []
        for i, (a, b) in enumerate(WAYS):
            rows = 24
            if phase == START:
                rows = 32 if b else 48
            if a:
                src = srows.at[phase, 0 if a > 0 else 1, :rows]
                dst = rrows.at[phase, i, :rows]
            else:
                src = scols.at[phase, i - 6]
                dst = rcols.at[phase, i - 6]
            plan.append(
                pltpu.make_async_remote_copy(
                    src, dst, hsend.at[phase], hrecv.at[phase],
                    device_id=(gx + a, gy + b), device_id_type=MESH,
                )
            )
        return plan

    count_x = has_x[1].astype(jnp.int32) + has_x[-1].astype(jnp.int32)
    count_y = has_y[1].astype(jnp.int32) + has_y[-1].astype(jnp.int32)

    halos = [halo_copies(phase) for phase in range(4)]

    def halo_start(phase, which):
        @pl.when(count_x + count_y == 4)
        def _():
            for i in which:
                halos[phase][i].start()

        @pl.when(count_x + count_y < 4)
        def _():
            for i in which:

                @pl.when(has(*WAYS[i]))
                def _(i=i):
                    halos[phase][i].start()

    def all_of(ref, sem):
        return pltpu.make_async_copy(ref, ref, sem)

    def halo_all(phase, sem):
        side, corner = (48, 32) if phase == START else (24, 24)
        flat = rrows.reshape(4 * 6 * 48, CN)
        for nx in (1, 2):
            for ny in (1, 2):
                rows = nx * side + nx * ny * corner + ny * 16

                @pl.when((count_x == nx) & (count_y == ny))
                def _(rows=rows):
                    all_of(flat.at[pl.ds(phase * 6 * 48, rows)], sem.at[phase]).wait()

    def halo_wait(phase):
        halo_all(phase, hrecv)

    def halo_sent(phase):
        halo_all(phase, hsend)

    def pack_rows(phase, flat, first, slab, pitch, fields):
        for f in range(fields):
            start = first + f * slab * pitch
            at = slot_of(f) * 8
            srows[phase, 0, at:at + 8, :] = flat[pl.ds(start + CE - 1, 8, stride=pitch), :]
            srows[phase, 1, at:at + 8, :] = flat[pl.ds(start, 8, stride=pitch), :]

    def pack_cols(phase, cells_at, fields, high, low):
        def pack(level, carry):
            high, low = carry
            for f in range(fields):
                cells = cells_at(f, level)
                place = slot_of(f) * 8 + level
                here = lane16 == place
                high = jnp.where(here, pltpu.roll(cells, place + 1, 1), high)
                low = jnp.where(here, pltpu.roll(cells, place, 1), low)
            return high, low

        for level in range(LEV):
            high, low = pack(level, (high, low))
        scols[phase, 0] = high
        scols[phase, 1] = low

    def flat_of(pad):
        return pad.reshape(pad.shape[0] * SLABS * PITCH, CN)

    def padded_cells(pad, first):
        return lambda f, level: pad[first + f, level + 1, 8:24, :]

    SIDES = ((4, 0, 1, -1, 7), (5, 2, 3, 1, 24))

    def take_rows(phase, f, masks):
        out = []
        for side, (own, left, right, a, row) in enumerate(SIDES):
            here = slice(slot_of(f) * 8, slot_of(f) * 8 + 8)
            middle = jnp.where(has(a, 0), rrows[phase, own, here, :], 0.0)
            minus = plus = jnp.zeros((8, 128), F32)
            if f < 3:
                minus = jnp.where(has(a, -1), rrows[phase, left, here, :], 0.0)
                plus = jnp.where(has(a, 1), rrows[phase, right, here, :], 0.0)
            for oi in range(masks):
                m, lo, hi = middle, minus, plus
                if masks > 1:
                    m = m * row_masks[own, oi]
                    lo = lo * row_masks[left, oi]
                    hi = hi * row_masks[right, oi]
                out.append((
                    side, oi, row, m,
                    pltpu.roll(jnp.where(lane8 == 127, lo, m), 1, 1),
                    pltpu.roll(jnp.where(lane8 == 0, hi, m), 127, 1),
                ))
        return out

    def store_rows(flats, index, row, values):
        where = pl.ds((index * SLABS + 1) * PITCH + row, 8, stride=PITCH)
        for flat, value in zip(flats, values):
            flat[where, :] = value

    def side_cols(phase):
        low = jnp.where(has(0, -1), rcols[phase, 0], 0.0)
        high = jnp.where(has(0, 1), rcols[phase, 1], 0.0)
        return low, high

    def turn(pads, first, fields):
        pad, pad_m, pad_p = pads

        def body(level, carry):
            for f in range(fields):
                cells = pad[first + f, level + 1, 8:24, :]
                pad_m[first + f, level + 1, 8:24, :] = pltpu.roll(cells, 1, 1)
                pad_p[first + f, level + 1, 8:24, :] = pltpu.roll(cells, 127, 1)
            return carry

        for level in range(LEV):
            body(level, 0)

    def take_edges(phase, pads, fields):
        _, pad_m, pad_p = pads
        flats = [flat_of(p) for p in pads]
        for f in range(fields):
            for _, _, row, m, lo, hi in take_rows(phase, f, 1):
                store_rows(flats, f, row, (m, lo, hi))
        low, high = side_cols(phase)

        def body(level, carry):
            for f in range(fields):
                place = slot_of(f) * 8 + level
                left = pltpu.roll(low, (128 - place) % 128, 1)
                right = pltpu.roll(high, 127 - place, 1)
                at_m = pad_m[f, level + 1, 8:24, :]
                at_p = pad_p[f, level + 1, 8:24, :]
                pad_m[f, level + 1, 8:24, :] = jnp.where(lane16 == 0, left, at_m)
                pad_p[f, level + 1, 8:24, :] = jnp.where(lane16 == 127, right, at_p)
            return carry

        for level in range(LEV):
            body(level, 0)

    pl.semaphore_wait(barrier, NX - 1 + NY - 1 + count_x * count_y)

    r1 = (r1_0, r1_1)

    stage1 = [
        [
            pltpu.make_async_remote_copy(
                pay_v.at[n], r1[n].at[pl.ds(gx * 3, 3)], send1.at[n], recv1.at[n],
                device_id=(x_at(d), gy), device_id_type=MESH,
            )
            for d in FAR_X
        ]
        for n in range(2)
    ]
    stage2 = [[], []]

    def line_start(n):
        for copy in stage1[n]:
            copy.start()
        r1[n][pl.ds(gx * 3, 3)] = pay_v[n]

    lane_half = lane8 < 64

    def slots_start(n):
        all_of(r1[n].at[0:3 * (NX - 1)], recv1.at[n]).wait()

        def fill(to, carry):
            halves = []
            for g in range(4):
                slot = to * 4 + g
                place = found_s[0, slot]
                first = r1[n][jnp.clip(found_s[1, slot], 0, 3 * NX - 1)]
                second = r1[n][jnp.clip(found_s[2, slot], 0, 3 * NX - 1)]
                second = pltpu.roll(second, found_s[3, slot], 1)
                out2[n, to, g * 8:(g + 1) * 8, :] = jnp.where(place > 0, first, 0.0)
                halves.append(jnp.where(place > 0, second, 0.0))
            for h in range(2):
                joined = jnp.where(lane_half, halves[2 * h], halves[2 * h + 1])
                out2[n, to, 32 + h * 8:40 + h * 8, :] = joined
            return carry

        for d in FAR_Y + (0,):
            to = y_at(d)
            fill(to, 0)
            if d == 0:
                continue
            copy = pltpu.make_async_remote_copy(
                out2.at[n, to], r2.at[n, gy], send2.at[n], recv2.at[n],
                device_id=(gx, to), device_id_type=MESH,
            )
            copy.start()
            stage2[n].append(copy)
        r2[n, gy] = out2[n, gy]

    line_start(0)
    for copy in copies_in[5:]:
        copy.wait()
    low_level = ranges_s[0, 0, 0]
    high_level = ranges_s[0, 0, 1]
    copies_in[1].wait()
    copies_in[2].wait()
    range_rows = jnp.where(sub8 == 0, low_level, high_level).astype(F32)
    pack_rows(START, flat_of(ku0), PITCH + 8, SLABS, PITCH, 5)
    for side in range(2):
        srows[START, side, 24:32, :] = range_rows
    range_cols = jnp.where(lane16 == 24, low_level, high_level).astype(F32)
    pack_cols(START, padded_cells(ku0, 0), 5, range_cols, range_cols)
    turn((ku0, kum, kup), 0, 5)

    halo_start(START, range(8))
    line_start(1)
    blank = jnp.zeros((PITCH, CN), F32)
    for pads, fields in (((ku0, kum, kup), 5), ((oi0, oim, oip), 12), ((md0, mdm, mdp), 3)):

        def clear(f, carry, pads=pads):
            for pad in pads:
                pad[f, 0] = blank
                pad[f, SLABS - 1] = blank
            return carry

        lax.fori_loop(0, fields, clear, 0)

    def find(slot, carry):
        place = jnp.int32(0)
        for x in range(NX):
            for k in range(2):
                named = route_s[(x * NY + gy) * 2 + k] == gx * 32 + slot
                place = jnp.maximum(place, jnp.where(named, 1 + 3 * x + k, 0))
        at = jnp.maximum(place - 1, 0)
        k = lax.rem(at, 3)
        found_s[0, slot] = place
        found_s[1, slot] = at
        found_s[2, slot] = at - k + 2
        found_s[3, slot] = 64 * lax.rem(k + slot, 2)
        return carry

    lax.fori_loop(0, NY * 4, find, 0)

    def hat25(cells, points):
        return jnp.maximum(25 - jnp.abs(4 * cells - 25 * points), 0).astype(F32)

    for g in range(4):
        for ref, count in ((east_a, 4), (east_b, 2)):
            shape = (16, count * 8)
            cells = iota(shape, 0) + offs_s[0, 1, 0, g]
            cols = iota(shape, 1)
            weights = hat25(cells, lax.rem(cols, 8))
            mine = lax.div(cols, 8) == (g if count == 4 else g // 2)
            ref[g * 16:(g + 1) * 16, :] = jnp.where(mine, weights, 0.0).astype(jnp.bfloat16)
        point = iota((128, 256), 0)
        cell = iota((128, 256), 1)
        north = hat25(lax.rem(cell, 128) + offs_s[0, 2, 0, g], lax.rem(point, 32)) * (1.0 / 625.0)
        depth = (offs_s[0, 0, 0, g] + lax.div(cell, 128)).astype(F32) * (4.0 / 25.0)
        upright = jnp.where(point < 32, 1.0 - depth, depth)
        keep = (point < 64) & (lax.rem(point, 32) < COARSE_NORTH)
        weights = jnp.where(keep, north * upright, 0.0)
        high = weights.astype(jnp.bfloat16)
        q_high[g] = high
        q_low[g] = (weights - high.astype(F32)).astype(jnp.bfloat16)

    slots_start(0)

    halo_wait(START)
    take_edges(START, (ku0, kum, kup), 5)
    level8 = sub8.astype(F32)
    for i in range(6):
        low = rrows[START, i, 24:25, :]
        high = rrows[START, i, 25:26, :]
        row_masks[i, 0] = jnp.where(level8 < low, 1.0, 0.0)
        row_masks[i, 1] = jnp.where((level8 >= low) & (level8 < high), 1.0, 0.0)
    ku = {-1: kum, 0: ku0, 1: kup}

    def prepare(level, carry):
        def get(f, shift):
            dl, de, dn = shift
            return ku[dn][f, level + 1 + dl, 8 + de:24 + de, :]

        mu = get(3, (0, 0, 0))
        stiff = get(4, (0, 0, 0)) + 2.0 * mu
        shear_sides = []
        stiff_sides = []
        for d in range(3):
            for s in range(2):
                shift = moved(d, 1 - 2 * s)
                mu_side = get(3, shift)
                a = 0.5 * (mu + mu_side)
                b = 0.5 * (stiff + (get(4, shift) + 2.0 * mu_side))
                coef[d * 2 + s, level] = a
                coef[6 + d * 2 + s, level] = b
                shear_sides.append(a)
                stiff_sides.append(b)
        for i in range(3):
            total = None
            for d in range(3):
                sides = stiff_sides if d == i else shear_sides
                part = sides[2 * d] + sides[2 * d + 1]
                total = part if total is None else total + part
            coef[12 + i, level] = total
        dens_v[level] = step_square / dens_v[level]
        return carry

    def elastic(level, pads, index):
        return elastic_at(level, pads, index, ku, coef)

    copies_in[4].wait()
    lax.fori_loop(0, LEV, prepare, 0)
    copies_in[3].wait()

    def first_base(level, carry):
        applied = elastic(level, ku, lambda c: c)
        scale = dens_v[level]
        for c in range(3):
            now = ku0[c, level + 1, 8:24, :]
            base[c, level] = 2.0 * now - prev_v[c, level] + scale * applied[c]
        return carry

    lax.fori_loop(0, LEV, first_base, 0)

    slots_start(1)

    def incident(n):
        all_of(r2.at[n, 0:NY - 1], recv2.at[n]).wait()
        got = r2[n, 0]
        for y in range(1, NY):
            got = got + r2[n, y]
        eastern_a = dot_exact(east_a[...], got[0:32])
        eastern_b = dot_exact(east_b[...], got[32:48])
        for g in range(4):
            piece_a = eastern_a[g * 16:(g + 1) * 16]
            piece_b = eastern_b[g * 16:(g + 1) * 16]
            if g % 2:
                piece_b = pltpu.roll(piece_b, 64, 1)
            pieces = [piece_a, pltpu.roll(piece_a, 64, 1), piece_b]
            high, middle, _ = split(jnp.concatenate(pieces, axis=0))
            both = jnp.dot(
                jnp.concatenate([high, middle], axis=0), q_high[g], preferred_element_type=F32
            )
            rest = jnp.dot(high, q_low[g], preferred_element_type=F32)
            fine = both[:48] + (both[48:] + rest)
            for j in range(2):
                for c in range(3):
                    inc_v[n, c, 2 * g + j] = fine[c * 16:(c + 1) * 16, j * 128:(j + 1) * 128]
        phase = FORCE_0 + n
        flat = inc_v.reshape(6 * LEV * CE, CN)
        pack_rows(phase, flat, n * 3 * LEV * CE, LEV, CE, 3)
        halo_start(phase, range(6))
        zero = jnp.zeros((16, 128), F32)
        pack_cols(phase, lambda f, level: inc_v[n, f, level], 3, zero, zero)
        halo_start(phase, (6, 7))

    def mask_inside(n):
        def body(level, carry):
            outer = (low_level > level).astype(F32)
            inner = ((low_level <= level) & (high_level > level)).astype(F32)
            for c in range(3):
                cells = inc_v[n, c, level]
                values = (cells, pltpu.roll(cells, 1, 1), pltpu.roll(cells, 127, 1))
                for pad, value in zip((oi0, oim, oip), values):
                    pad[n * 6 + c, level + 1, 8:24, :] = outer * value
                    pad[n * 6 + 3 + c, level + 1, 8:24, :] = inner * value
            return carry

        for level in range(LEV):
            body(level, 0)

    def take_masked(n):
        phase = FORCE_0 + n
        halo_wait(phase)
        flats = [flat_of(p) for p in (oi0, oim, oip)]
        for c in range(3):
            for _, oi, row, m, lo, hi in take_rows(phase, c, 2):
                store_rows(flats, n * 6 + oi * 3 + c, row, (m, lo, hi))
        low, high = side_cols(phase)
        bounds = []
        for side in range(2):
            got = rcols[START, side]
            bounds.append([
                jnp.broadcast_to(got[:, 24 + b:25 + b], (16, 128)) for b in range(2)
            ])

        def body(level, carry):
            here = float(level)
            outer = [here < bounds[side][0] for side in range(2)]
            inner = [(here >= bounds[side][0]) & (here < bounds[side][1]) for side in range(2)]
            for c in range(3):
                place = c * 8 + level
                left = pltpu.roll(low, (128 - place) % 128, 1)
                right = pltpu.roll(high, 127 - place, 1)
                for oi, masks in ((0, outer), (1, inner)):
                    at = n * 6 + oi * 3 + c
                    at_m = oim[at, level + 1, 8:24, :]
                    at_p = oip[at, level + 1, 8:24, :]
                    new_m = jnp.where(masks[0], left, 0.0)
                    new_p = jnp.where(masks[1], right, 0.0)
                    oim[at, level + 1, 8:24, :] = jnp.where(lane16 == 0, new_m, at_m)
                    oip[at, level + 1, 8:24, :] = jnp.where(lane16 == 127, new_p, at_p)
            return carry

        for level in range(LEV):
            body(level, 0)

    incident(0)
    mask_inside(0)
    incident(1)

    oi = {-1: oim, 0: oi0, 1: oip}
    md = {-1: mdm, 0: md0, 1: mdp}

    def force(level, n):
        inside = (level >= low_level) & (level < high_level)
        which = n * 6 + jnp.where(inside, 0, 3)
        sign = inside.astype(F32) - (level < low_level).astype(F32)
        return sign, elastic(level, oi, lambda c: which + c)

    take_masked(0)

    def middle(level, carry):
        sign, applied = force(level, 0)
        scale = sign * dens_v[level]
        for c in range(3):
            cells = base[c, level] + scale * applied[c]
            md0[c, level + 1, 8:24, :] = cells
            mid_v[c, level] = cells
        return carry

    lax.fori_loop(0, LEV, middle, 0, unroll=2)
    pack_rows(MIDDLE, flat_of(md0), PITCH + 8, SLABS, PITCH, 3)
    halo_start(MIDDLE, range(6))
    zero = jnp.zeros((16, 128), F32)
    pack_cols(MIDDLE, padded_cells(md0, 0), 3, zero, zero)
    halo_start(MIDDLE, (6, 7))
    mask_inside(1)
    turn((md0, mdm, mdp), 0, 3)
    take_masked(1)

    def second_base(level, carry):
        sign, applied = force(level, 1)
        scale = sign * dens_v[level]
        for c in range(3):
            mid = md0[c, level + 1, 8:24, :]
            now = ku0[c, level + 1, 8:24, :]
            base[c, level] = 2.0 * mid - now + scale * applied[c]
        return carry

    lax.fori_loop(0, LEV, second_base, 0)
    for n in range(2):
        all_of(r1[n].at[0:3 * (NX - 1)], send1.at[n]).wait()
        all_of(r2.at[n, 0:NY - 1], send2.at[n]).wait()
    for phase in (START, FORCE_0, FORCE_1):
        halo_sent(phase)
    halo_wait(MIDDLE)
    take_edges(MIDDLE, (md0, mdm, mdp), 3)

    halo_sent(MIDDLE)


def finish(
    inc_v, mid_v, ku0, kum, kup, md0, mdm, mdp, coef, base, dens_v,
    inc_h, mid_h, nxt_h, nxt_v, sems,
):
    copies = [
        pltpu.make_async_copy(inc_v, inc_h, sems.at[0]),
        pltpu.make_async_copy(mid_v, mid_h, sems.at[1]),
    ]
    for copy in copies:
        copy.start()
    ku = {-1: kum, 0: ku0, 1: kup}
    md = {-1: mdm, 0: md0, 1: mdp}

    def last(level, carry):
        applied = elastic_at(level, md, lambda c: c, ku, coef)
        scale = dens_v[level]
        for c in range(3):
            nxt_v[c, level] = base[c, level] + scale * applied[c]
        return carry

    for part in range(PARTS):
        levels = LEV // PARTS
        lax.fori_loop(part * levels, (part + 1) * levels, last, 0, unroll=2)
        here = pl.ds(part * levels, levels)
        copy = pltpu.make_async_copy(nxt_v.at[:, here], nxt_h.at[:, here], sems.at[2 + part])
        copy.start()
        copies.append(copy)
    for copy in copies:
        copy.wait()


def local(disp_now, disp_prev, density, moduli, coarse, block_route, ranges, offsets):
    hbm = pl.BlockSpec(memory_space=pl.ANY)
    on_chip = pl.BlockSpec(memory_space=pltpu.VMEM)

    def vmem(*shape):
        return pltpu.VMEM(shape, F32)

    dma = pltpu.SemaphoreType.DMA
    outs = (
        jax.ShapeDtypeStruct((2, 3, LEV, CE, CN), F32),
        jax.ShapeDtypeStruct((3, LEV, CE, CN), F32),
        jax.ShapeDtypeStruct((3, LEV, CE, CN), F32),
    )
    def array(*shape):
        return jax.ShapeDtypeStruct(shape, F32)

    held = (
        *outs[:2],
        *[array(5, SLABS, PITCH, CN)] * 3,
        *[array(3, SLABS, PITCH, CN)] * 3,
        array(15, LEV, CE, CN), array(3, LEV, CE, CN), array(LEV, CE, CN),
    )
    args = (
        disp_now, disp_prev, density, moduli, coarse, block_route, ranges,
        offsets.transpose(0, 3, 1, 2),
    )
    results = pl.pallas_call(
        kernel,
        out_shape=held,
        in_specs=[hbm] * 8,
        out_specs=(on_chip,) * len(held),
        scratch_shapes=[
            pltpu.SMEM((256,), jnp.int32), pltpu.SMEM((1, 1, 2), jnp.int32),
            pltpu.SMEM((1, 3, 1, 4), jnp.int32),
            vmem(3, LEV, CE, CN), vmem(2, 24, 256), vmem(24, 256),
            vmem(192, 128), pltpu.SMEM((4, NY * 4), jnp.int32),
            vmem(2, 3, 8, 128), vmem(NX * 3, 8, 128), vmem(NX * 3, 8, 128),
            vmem(2, NY, 48, 128), vmem(2, NY, 48, 128),
            pltpu.VMEM((64, 32), jnp.bfloat16), pltpu.VMEM((64, 16), jnp.bfloat16),
            pltpu.VMEM((4, 128, 256), jnp.bfloat16), pltpu.VMEM((4, 128, 256), jnp.bfloat16),
            *[vmem(12, SLABS, PITCH, CN)] * 3,
            vmem(4, 2, 48, 128), vmem(4, 2, 16, 128),
            vmem(4, 6, 48, 128), vmem(4, 2, 16, 128), vmem(6, 2, 8, 128),
            dma((4,)), dma((4,)), dma((2,)), dma((2,)), dma((2,)), dma((2,)),
            dma((8,)),
        ],
        compiler_params=pltpu.CompilerParams(
            collective_id=0, has_side_effects=True, vmem_limit_bytes=40 * 1024 * 1024
        ),
    )(*[pltpu.with_memory_space_constraint(v, pltpu.HBM) for v in args])
    return pl.pallas_call(
        finish,
        out_shape=outs,
        in_specs=[on_chip] * len(held),
        out_specs=(hbm, hbm, hbm),
        scratch_shapes=[vmem(3, LEV, CE, CN), dma((2 + PARTS,))],
        compiler_params=pltpu.CompilerParams(vmem_limit_bytes=4 * 1024 * 1024),
    )(*results)


def solution(mesh):
    return jax.shard_map(
        local,
        mesh=mesh,
        in_specs=(
            P(None, None, "gx", "gy"),
            P(None, None, "gx", "gy"),
            P(None, "gx", "gy"),
            P(None, None, "gx", "gy"),
            P(("gx", "gy"), None, None),
            P(),
            P("gx", "gy", None),
            P("gx", "gy", None, None),
        ),
        out_specs=(
            P(None, None, None, "gx", "gy"),
            P(None, None, "gx", "gy"),
            P(None, None, "gx", "gy"),
        ),
        check_vma=False,
    )
```

```python
import jax
import jax.numpy as jnp
from jax import lax
from jax.experimental import pallas as pl
from jax.experimental.pallas import tpu as pltpu
from jax.sharding import PartitionSpec as P

step_square = 0.05
time_weights = ((-0.0595, 0.7735, 0.3315, -0.0455), (-0.063756, 0.607068, 0.517132, -0.060444))
NX, NY = 16, 8
LEV, CE, CN = 8, 16, 128
SLABS, PITCH = LEV + 2, 32
COARSE_EAST, COARSE_NORTH = 8, 26
MESH = pl.DeviceIdType.MESH
PARTS = 4
FAR_X = (10, 9, 11, 6, 14, 7, 5, 13, 15, 8, 2, 4, 12, 1, 3)
FAR_Y = (4, 3, 5, 2, 6, 1, 7)
F32 = jnp.float32
START, FORCE_0, FORCE_1, MIDDLE = range(4)


def iota(shape, dim):
    return lax.broadcasted_iota(jnp.int32, shape, dim)


def split(x):
    high = x.astype(jnp.bfloat16)
    rest = x - high.astype(F32)
    middle = rest.astype(jnp.bfloat16)
    low = (rest - middle.astype(F32)).astype(jnp.bfloat16)
    return high, middle, low


def dot_exact(whole, x):
    parts = [jnp.dot(whole, part, preferred_element_type=F32) for part in split(x)]
    return (parts[2] + parts[1]) + parts[0]


steps = ((1, 0, 0), (0, 1, 0), (0, 0, 1))


def moved(d, sign):
    return tuple(sign * s for s in steps[d])


def elastic_at(level, pads, index, ku, coef):
    cache = {}

    def get(c, shift):
        key = (c, shift)
        if key not in cache:
            dl, de, dn = shift
            cache[key] = pads[dn][index(c), level + 1 + dl, 8 + de:24 + de, :]
        return cache[key]

    kcache = {}

    def modulus(f, shift):
        key = (f, shift)
        if key not in kcache:
            dl, de, dn = shift
            kcache[key] = ku[dn][f, level + 1 + dl, 8 + de:24 + de, :]
        return kcache[key]

    def both(i, si, j, sj):
        a, b = moved(i, si), moved(j, sj)
        return tuple(p + q for p, q in zip(a, b))

    results = []
    for i in range(3):
        total = -coef[12 + i, level] * get(i, (0, 0, 0))
        for d in range(3):
            for s in range(2):
                at = (6 if d == i else 0) + d * 2 + s
                total = total + coef[at, level] * get(i, moved(d, 1 - 2 * s))
        mixed = None
        for j in range(3):
            if j == i:
                continue
            pp = get(j, both(i, 1, j, 1))
            pm = get(j, both(i, 1, j, -1))
            mp = get(j, both(i, -1, j, 1))
            mm = get(j, both(i, -1, j, -1))
            part = (
                modulus(4, moved(i, 1)) * (pp - pm)
                - modulus(4, moved(i, -1)) * (mp - mm)
                + modulus(3, moved(j, 1)) * (pp - mp)
                - modulus(3, moved(j, -1)) * (pm - mm)
            )
            mixed = part if mixed is None else mixed + part
        results.append(total + 0.25 * mixed)
    return results


def kernel(
    now_h, prev_h, dens_h, mod_h, coarse_h, route_h, ranges_h, offs_h,
    inc_v, mid_v, ku0, kum, kup, md0, mdm, mdp, coef, base, dens_v,
    route_s, ranges_s, offs_s, prev_v, coarse_v, timed_v, turned_v,
    found_s, pay_v, r1_0, r1_1, out2, r2, east_a, east_b, q_high, q_low,
    oi0, oim, oip, srows, scols, rrows, rcols, row_masks,
    hsend, hrecv, send1, recv1, send2, recv2, local_sem,
):
    gx = lax.axis_index("gx")
    gy = lax.axis_index("gy")

    def x_at(d):
        return lax.rem(gx + (d + NX), NX)

    def y_at(d):
        return lax.rem(gy + (d + NY), NY)

    has_x = {1: gx < NX - 1, -1: gx > 0, 0: None}
    has_y = {1: gy < NY - 1, -1: gy > 0, 0: None}

    def has(a, b):
        if a and b:
            return has_x[a] & has_y[b]
        return has_x[a] if a else has_y[b]

    copies_in = [
        pltpu.make_async_copy(coarse_h, coarse_v, local_sem.at[0]),
        pltpu.make_async_copy(mod_h, ku0.at[3:5, 1:9, 8:24, :], local_sem.at[1]),
        pltpu.make_async_copy(now_h, ku0.at[0:3, 1:9, 8:24, :], local_sem.at[2]),
        pltpu.make_async_copy(prev_h, prev_v, local_sem.at[3]),
        pltpu.make_async_copy(dens_h, dens_v, local_sem.at[4]),
        pltpu.make_async_copy(route_h, route_s, local_sem.at[5]),
        pltpu.make_async_copy(ranges_h, ranges_s, local_sem.at[6]),
        pltpu.make_async_copy(offs_h, offs_s, local_sem.at[7]),
    ]
    for at in (0, 1, 2):
        copies_in[at].start()

    barrier = pltpu.get_barrier_semaphore()
    for d in range(1, NX):
        pl.semaphore_signal(barrier, inc=1, device_id=(x_at(d), gy), device_id_type=MESH)
    for d in range(1, NY):
        pl.semaphore_signal(barrier, inc=1, device_id=(gx, y_at(d)), device_id_type=MESH)
    for a in (-1, 1):
        for b in (-1, 1):

            @pl.when(has(a, b))
            def _(a=a, b=b):
                pl.semaphore_signal(
                    barrier, inc=1, device_id=(gx + a, gy + b), device_id_type=MESH
                )

    for at in (5, 6, 7, 3, 4):
        copies_in[at].start()

    lane8 = iota((8, 128), 1)
    sub8 = iota((8, 128), 0)
    lane16 = iota((16, 128), 1)

    copies_in[0].wait()
    for n in range(2):
        for k in range(2):
            row = (n * 2 + k) * 6
            total = None
            for t in range(4):
                term = time_weights[n][t] * coarse_v[k, t * 6:t * 6 + 6, :]
                total = term if total is None else total + term
            timed_v[row:row + 6, :] = total
    timed = timed_v[...]
    for a in range(COARSE_EAST):
        shifted = timed if a == 0 else pltpu.roll(timed, 256 - COARSE_NORTH * a, 1)
        turned_v[a * 24:(a + 1) * 24, :] = shifted[:, :128]
    for n in range(2):
        places = [[(n * 2 + k) * 6 + p for p in range(4)] for k in range(2)]
        places.append([(n * 2 + k) * 6 + p for k in range(2) for p in (4, 5)])
        for at, rows in enumerate(places):
            joined = None
            for part, row in enumerate(rows):
                piece = turned_v[pl.ds(row, 8, stride=24), :]
                if part:
                    piece = pltpu.roll(piece, part * 32, 1)
                here = (lane8 >= part * 32) & (lane8 < part * 32 + COARSE_NORTH)
                joined = jnp.where(here, piece, 0.0 if joined is None else joined)
            pay_v[n, at] = joined

    WAYS = ((1, 1), (1, -1), (-1, 1), (-1, -1), (1, 0), (-1, 0), (0, 1), (0, -1))

    def slot_of(f):
        return f if f < 3 else f + 1

    def halo_copies(phase):
        plan = []
        for i, (a, b) in enumerate(WAYS):
            rows = 24
            if phase == START:
                rows = 32 if b else 48
            if a:
                src = srows.at[phase, 0 if a > 0 else 1, :rows]
                dst = rrows.at[phase, i, :rows]
            else:
                src = scols.at[phase, i - 6]
                dst = rcols.at[phase, i - 6]
            plan.append(
                pltpu.make_async_remote_copy(
                    src, dst, hsend.at[phase], hrecv.at[phase],
                    device_id=(gx + a, gy + b), device_id_type=MESH,
                )
            )
        return plan

    count_x = has_x[1].astype(jnp.int32) + has_x[-1].astype(jnp.int32)
    count_y = has_y[1].astype(jnp.int32) + has_y[-1].astype(jnp.int32)

    halos = [halo_copies(phase) for phase in range(4)]

    def halo_start(phase, which):
        @pl.when(count_x + count_y == 4)
        def _():
            for i in which:
                halos[phase][i].start()

        @pl.when(count_x + count_y < 4)
        def _():
            for i in which:

                @pl.when(has(*WAYS[i]))
                def _(i=i):
                    halos[phase][i].start()

    def all_of(ref, sem):
        return pltpu.make_async_copy(ref, ref, sem)

    def halo_all(phase, sem):
        side, corner = (48, 32) if phase == START else (24, 24)
        flat = rrows.reshape(4 * 6 * 48, CN)
        for nx in (1, 2):
            for ny in (1, 2):
                rows = nx * side + nx * ny * corner + ny * 16

                @pl.when((count_x == nx) & (count_y == ny))
                def _(rows=rows):
                    all_of(flat.at[pl.ds(phase * 6 * 48, rows)], sem.at[phase]).wait()

    def halo_wait(phase):
        halo_all(phase, hrecv)

    def halo_sent(phase):
        halo_all(phase, hsend)

    def pack_rows(phase, flat, first, slab, pitch, fields):
        for f in range(fields):
            start = first + f * slab * pitch
            at = slot_of(f) * 8
            srows[phase, 0, at:at + 8, :] = flat[pl.ds(start + CE - 1, 8, stride=pitch), :]
            srows[phase, 1, at:at + 8, :] = flat[pl.ds(start, 8, stride=pitch), :]

    def pack_cols(phase, cells_at, fields, high, low):
        def pack(level, carry):
            high, low = carry
            for f in range(fields):
                cells = cells_at(f, level)
                place = slot_of(f) * 8 + level
                here = lane16 == place
                high = jnp.where(here, pltpu.roll(cells, place + 1, 1), high)
                low = jnp.where(here, pltpu.roll(cells, place, 1), low)
            return high, low

        for level in range(LEV):
            high, low = pack(level, (high, low))
        scols[phase, 0] = high
        scols[phase, 1] = low

    def flat_of(pad):
        return pad.reshape(pad.shape[0] * SLABS * PITCH, CN)

    def padded_cells(pad, first):
        return lambda f, level: pad[first + f, level + 1, 8:24, :]

    SIDES = ((4, 0, 1, -1, 7), (5, 2, 3, 1, 24))

    def take_rows(phase, f, masks):
        out = []
        for side, (own, left, right, a, row) in enumerate(SIDES):
            here = slice(slot_of(f) * 8, slot_of(f) * 8 + 8)
            middle = jnp.where(has(a, 0), rrows[phase, own, here, :], 0.0)
            minus = plus = jnp.zeros((8, 128), F32)
            if f < 3:
                minus = jnp.where(has(a, -1), rrows[phase, left, here, :], 0.0)
                plus = jnp.where(has(a, 1), rrows[phase, right, here, :], 0.0)
            for oi in range(masks):
                m, lo, hi = middle, minus, plus
                if masks > 1:
                    m = m * row_masks[own, oi]
                    lo = lo * row_masks[left, oi]
                    hi = hi * row_masks[right, oi]
                out.append((
                    side, oi, row, m,
                    pltpu.roll(jnp.where(lane8 == 127, lo, m), 1, 1),
                    pltpu.roll(jnp.where(lane8 == 0, hi, m), 127, 1),
                ))
        return out

    def store_rows(flats, index, row, values):
        where = pl.ds((index * SLABS + 1) * PITCH + row, 8, stride=PITCH)
        for flat, value in zip(flats, values):
            flat[where, :] = value

    def side_cols(phase):
        low = jnp.where(has(0, -1), rcols[phase, 0], 0.0)
        high = jnp.where(has(0, 1), rcols[phase, 1], 0.0)
        return low, high

    def turn(pads, first, fields):
        pad, pad_m, pad_p = pads

        def body(level, carry):
            for f in range(fields):
                cells = pad[first + f, level + 1, 8:24, :]
                pad_m[first + f, level + 1, 8:24, :] = pltpu.roll(cells, 1, 1)
                pad_p[first + f, level + 1, 8:24, :] = pltpu.roll(cells, 127, 1)
            return carry

        for level in range(LEV):
            body(level, 0)

    def take_edges(phase, pads, fields):
        _, pad_m, pad_p = pads
        flats = [flat_of(p) for p in pads]
        for f in range(fields):
            for _, _, row, m, lo, hi in take_rows(phase, f, 1):
                store_rows(flats, f, row, (m, lo, hi))
        low, high = side_cols(phase)

        def body(level, carry):
            for f in range(fields):
                place = slot_of(f) * 8 + level
                left = pltpu.roll(low, (128 - place) % 128, 1)
                right = pltpu.roll(high, 127 - place, 1)
                at_m = pad_m[f, level + 1, 8:24, :]
                at_p = pad_p[f, level + 1, 8:24, :]
                pad_m[f, level + 1, 8:24, :] = jnp.where(lane16 == 0, left, at_m)
                pad_p[f, level + 1, 8:24, :] = jnp.where(lane16 == 127, right, at_p)
            return carry

        for level in range(LEV):
            body(level, 0)

    pl.semaphore_wait(barrier, NX - 1 + NY - 1 + count_x * count_y)

    r1 = (r1_0, r1_1)

    stage1 = [
        [
            pltpu.make_async_remote_copy(
                pay_v.at[n], r1[n].at[pl.ds(gx * 3, 3)], send1.at[n], recv1.at[n],
                device_id=(x_at(d), gy), device_id_type=MESH,
            )
            for d in FAR_X
        ]
        for n in range(2)
    ]
    stage2 = [[], []]

    def line_start(n):
        for copy in stage1[n]:
            copy.start()
        r1[n][pl.ds(gx * 3, 3)] = pay_v[n]

    lane_half = lane8 < 64

    def slots_start(n):
        all_of(r1[n].at[0:3 * (NX - 1)], recv1.at[n]).wait()

        def fill(to, carry):
            halves = []
            for g in range(4):
                slot = to * 4 + g
                place = found_s[0, slot]
                first = r1[n][jnp.clip(found_s[1, slot], 0, 3 * NX - 1)]
                second = r1[n][jnp.clip(found_s[2, slot], 0, 3 * NX - 1)]
                second = pltpu.roll(second, found_s[3, slot], 1)
                out2[n, to, g * 8:(g + 1) * 8, :] = jnp.where(place > 0, first, 0.0)
                halves.append(jnp.where(place > 0, second, 0.0))
            for h in range(2):
                joined = jnp.where(lane_half, halves[2 * h], halves[2 * h + 1])
                out2[n, to, 32 + h * 8:40 + h * 8, :] = joined
            return carry

        for d in FAR_Y + (0,):
            to = y_at(d)
            fill(to, 0)
            if d == 0:
                continue
            copy = pltpu.make_async_remote_copy(
                out2.at[n, to], r2.at[n, gy], send2.at[n], recv2.at[n],
                device_id=(gx, to), device_id_type=MESH,
            )
            copy.start()
            stage2[n].append(copy)
        r2[n, gy] = out2[n, gy]

    line_start(0)
    for copy in copies_in[5:]:
        copy.wait()
    low_level = ranges_s[0, 0, 0]
    high_level = ranges_s[0, 0, 1]
    copies_in[1].wait()
    copies_in[2].wait()
    range_rows = jnp.where(sub8 == 0, low_level, high_level).astype(F32)
    pack_rows(START, flat_of(ku0), PITCH + 8, SLABS, PITCH, 5)
    for side in range(2):
        srows[START, side, 24:32, :] = range_rows
    range_cols = jnp.where(lane16 == 24, low_level, high_level).astype(F32)
    pack_cols(START, padded_cells(ku0, 0), 5, range_cols, range_cols)
    turn((ku0, kum, kup), 0, 5)

    halo_start(START, range(8))
    line_start(1)
    blank = jnp.zeros((PITCH, CN), F32)
    for pads, fields in (((ku0, kum, kup), 5), ((oi0, oim, oip), 12), ((md0, mdm, mdp), 3)):

        def clear(f, carry, pads=pads):
            for pad in pads:
                pad[f, 0] = blank
                pad[f, SLABS - 1] = blank
            return carry

        lax.fori_loop(0, fields, clear, 0)

    def find(slot, carry):
        place = jnp.int32(0)
        for x in range(NX):
            for k in range(2):
                named = route_s[(x * NY + gy) * 2 + k] == gx * 32 + slot
                place = jnp.maximum(place, jnp.where(named, 1 + 3 * x + k, 0))
        at = jnp.maximum(place - 1, 0)
        k = lax.rem(at, 3)
        found_s[0, slot] = place
        found_s[1, slot] = at
        found_s[2, slot] = at - k + 2
        found_s[3, slot] = 64 * lax.rem(k + slot, 2)
        return carry

    lax.fori_loop(0, NY * 4, find, 0)

    def hat25(cells, points):
        return jnp.maximum(25 - jnp.abs(4 * cells - 25 * points), 0).astype(F32)

    for g in range(4):
        for ref, count in ((east_a, 4), (east_b, 2)):
            shape = (16, count * 8)
            cells = iota(shape, 0) + offs_s[0, 1, 0, g]
            cols = iota(shape, 1)
            weights = hat25(cells, lax.rem(cols, 8))
            mine = lax.div(cols, 8) == (g if count == 4 else g // 2)
            ref[g * 16:(g + 1) * 16, :] = jnp.where(mine, weights, 0.0).astype(jnp.bfloat16)
        point = iota((128, 256), 0)
        cell = iota((128, 256), 1)
        north = hat25(lax.rem(cell, 128) + offs_s[0, 2, 0, g], lax.rem(point, 32)) * (1.0 / 625.0)
        depth = (offs_s[0, 0, 0, g] + lax.div(cell, 128)).astype(F32) * (4.0 / 25.0)
        upright = jnp.where(point < 32, 1.0 - depth, depth)
        keep = (point < 64) & (lax.rem(point, 32) < COARSE_NORTH)
        weights = jnp.where(keep, north * upright, 0.0)
        high = weights.astype(jnp.bfloat16)
        q_high[g] = high
        q_low[g] = (weights - high.astype(F32)).astype(jnp.bfloat16)

    slots_start(0)

    halo_wait(START)
    take_edges(START, (ku0, kum, kup), 5)
    level8 = sub8.astype(F32)
    for i in range(6):
        low = rrows[START, i, 24:25, :]
        high = rrows[START, i, 25:26, :]
        row_masks[i, 0] = jnp.where(level8 < low, 1.0, 0.0)
        row_masks[i, 1] = jnp.where((level8 >= low) & (level8 < high), 1.0, 0.0)
    ku = {-1: kum, 0: ku0, 1: kup}

    def prepare(level, carry):
        def get(f, shift):
            dl, de, dn = shift
            return ku[dn][f, level + 1 + dl, 8 + de:24 + de, :]

        mu = get(3, (0, 0, 0))
        stiff = get(4, (0, 0, 0)) + 2.0 * mu
        shear_sides = []
        stiff_sides = []
        for d in range(3):
            for s in range(2):
                shift = moved(d, 1 - 2 * s)
                mu_side = get(3, shift)
                a = 0.5 * (mu + mu_side)
                b = 0.5 * (stiff + (get(4, shift) + 2.0 * mu_side))
                coef[d * 2 + s, level] = a
                coef[6 + d * 2 + s, level] = b
                shear_sides.append(a)
                stiff_sides.append(b)
        for i in range(3):
            total = None
            for d in range(3):
                sides = stiff_sides if d == i else shear_sides
                part = sides[2 * d] + sides[2 * d + 1]
                total = part if total is None else total + part
            coef[12 + i, level] = total
        dens_v[level] = step_square / dens_v[level]
        return carry

    def elastic(level, pads, index):
        return elastic_at(level, pads, index, ku, coef)

    copies_in[4].wait()
    lax.fori_loop(0, LEV, prepare, 0)
    copies_in[3].wait()

    def first_base(level, carry):
        applied = elastic(level, ku, lambda c: c)
        scale = dens_v[level]
        for c in range(3):
            now = ku0[c, level + 1, 8:24, :]
            base[c, level] = 2.0 * now - prev_v[c, level] + scale * applied[c]
        return carry

    lax.fori_loop(0, LEV, first_base, 0)

    slots_start(1)

    def incident(n):
        all_of(r2.at[n, 0:NY - 1], recv2.at[n]).wait()
        got = r2[n, 0]
        for y in range(1, NY):
            got = got + r2[n, y]
        eastern_a = dot_exact(east_a[...], got[0:32])
        eastern_b = dot_exact(east_b[...], got[32:48])
        for g in range(4):
            piece_a = eastern_a[g * 16:(g + 1) * 16]
            piece_b = eastern_b[g * 16:(g + 1) * 16]
            if g % 2:
                piece_b = pltpu.roll(piece_b, 64, 1)
            pieces = [piece_a, pltpu.roll(piece_a, 64, 1), piece_b]
            high, middle, _ = split(jnp.concatenate(pieces, axis=0))
            both = jnp.dot(
                jnp.concatenate([high, middle], axis=0), q_high[g], preferred_element_type=F32
            )
            rest = jnp.dot(high, q_low[g], preferred_element_type=F32)
            fine = both[:48] + (both[48:] + rest)
            for j in range(2):
                for c in range(3):
                    inc_v[n, c, 2 * g + j] = fine[c * 16:(c + 1) * 16, j * 128:(j + 1) * 128]
        phase = FORCE_0 + n
        flat = inc_v.reshape(6 * LEV * CE, CN)
        pack_rows(phase, flat, n * 3 * LEV * CE, LEV, CE, 3)
        halo_start(phase, range(6))
        zero = jnp.zeros((16, 128), F32)
        pack_cols(phase, lambda f, level: inc_v[n, f, level], 3, zero, zero)
        halo_start(phase, (6, 7))

    def mask_inside(n):
        def body(level, carry):
            outer = (low_level > level).astype(F32)
            inner = ((low_level <= level) & (high_level > level)).astype(F32)
            for c in range(3):
                cells = inc_v[n, c, level]
                values = (cells, pltpu.roll(cells, 1, 1), pltpu.roll(cells, 127, 1))
                for pad, value in zip((oi0, oim, oip), values):
                    pad[n * 6 + c, level + 1, 8:24, :] = outer * value
                    pad[n * 6 + 3 + c, level + 1, 8:24, :] = inner * value
            return carry

        for level in range(LEV):
            body(level, 0)

    def take_masked(n):
        phase = FORCE_0 + n
        halo_wait(phase)
        flats = [flat_of(p) for p in (oi0, oim, oip)]
        for c in range(3):
            for _, oi, row, m, lo, hi in take_rows(phase, c, 2):
                store_rows(flats, n * 6 + oi * 3 + c, row, (m, lo, hi))
        low, high = side_cols(phase)
        bounds = []
        for side in range(2):
            got = rcols[START, side]
            bounds.append([
                jnp.broadcast_to(got[:, 24 + b:25 + b], (16, 128)) for b in range(2)
            ])

        def body(level, carry):
            here = float(level)
            outer = [here < bounds[side][0] for side in range(2)]
            inner = [(here >= bounds[side][0]) & (here < bounds[side][1]) for side in range(2)]
            for c in range(3):
                place = c * 8 + level
                left = pltpu.roll(low, (128 - place) % 128, 1)
                right = pltpu.roll(high, 127 - place, 1)
                for oi, masks in ((0, outer), (1, inner)):
                    at = n * 6 + oi * 3 + c
                    at_m = oim[at, level + 1, 8:24, :]
                    at_p = oip[at, level + 1, 8:24, :]
                    new_m = jnp.where(masks[0], left, 0.0)
                    new_p = jnp.where(masks[1], right, 0.0)
                    oim[at, level + 1, 8:24, :] = jnp.where(lane16 == 0, new_m, at_m)
                    oip[at, level + 1, 8:24, :] = jnp.where(lane16 == 127, new_p, at_p)
            return carry

        for level in range(LEV):
            body(level, 0)

    incident(0)
    mask_inside(0)
    incident(1)
    mask_inside(1)

    oi = {-1: oim, 0: oi0, 1: oip}
    md = {-1: mdm, 0: md0, 1: mdp}

    def force(level, n):
        inside = (level >= low_level) & (level < high_level)
        which = n * 6 + jnp.where(inside, 0, 3)
        sign = inside.astype(F32) - (level < low_level).astype(F32)
        return sign, elastic(level, oi, lambda c: which + c)

    take_masked(0)

    def middle(level, carry):
        sign, applied = force(level, 0)
        scale = sign * dens_v[level]
        for c in range(3):
            cells = base[c, level] + scale * applied[c]
            md0[c, level + 1, 8:24, :] = cells
            mid_v[c, level] = cells
        return carry

    lax.fori_loop(0, LEV, middle, 0, unroll=2)
    pack_rows(MIDDLE, flat_of(md0), PITCH + 8, SLABS, PITCH, 3)
    halo_start(MIDDLE, range(6))
    zero = jnp.zeros((16, 128), F32)
    pack_cols(MIDDLE, padded_cells(md0, 0), 3, zero, zero)
    halo_start(MIDDLE, (6, 7))
    turn((md0, mdm, mdp), 0, 3)
    take_masked(1)

    def second_base(level, carry):
        sign, applied = force(level, 1)
        scale = sign * dens_v[level]
        for c in range(3):
            mid = md0[c, level + 1, 8:24, :]
            now = ku0[c, level + 1, 8:24, :]
            base[c, level] = 2.0 * mid - now + scale * applied[c]
        return carry

    lax.fori_loop(0, LEV, second_base, 0)
    for n in range(2):
        all_of(r1[n].at[0:3 * (NX - 1)], send1.at[n]).wait()
        all_of(r2.at[n, 0:NY - 1], send2.at[n]).wait()
    for phase in (START, FORCE_0, FORCE_1):
        halo_sent(phase)
    halo_wait(MIDDLE)
    take_edges(MIDDLE, (md0, mdm, mdp), 3)

    halo_sent(MIDDLE)


def finish(
    inc_v, mid_v, ku0, kum, kup, md0, mdm, mdp, coef, base, dens_v,
    inc_h, mid_h, nxt_h, nxt_v, sems,
):
    copies = [
        pltpu.make_async_copy(inc_v, inc_h, sems.at[0]),
        pltpu.make_async_copy(mid_v, mid_h, sems.at[1]),
    ]
    for copy in copies:
        copy.start()
    ku = {-1: kum, 0: ku0, 1: kup}
    md = {-1: mdm, 0: md0, 1: mdp}

    def last(level, carry):
        applied = elastic_at(level, md, lambda c: c, ku, coef)
        scale = dens_v[level]
        for c in range(3):
            nxt_v[c, level] = base[c, level] + scale * applied[c]
        return carry

    for part in range(PARTS):
        levels = LEV // PARTS
        lax.fori_loop(part * levels, (part + 1) * levels, last, 0, unroll=2)
        here = pl.ds(part * levels, levels)
        copy = pltpu.make_async_copy(nxt_v.at[:, here], nxt_h.at[:, here], sems.at[2 + part])
        copy.start()
        copies.append(copy)
    for copy in copies:
        copy.wait()


def local(disp_now, disp_prev, density, moduli, coarse, block_route, ranges, offsets):
    hbm = pl.BlockSpec(memory_space=pl.ANY)
    on_chip = pl.BlockSpec(memory_space=pltpu.VMEM)

    def vmem(*shape):
        return pltpu.VMEM(shape, F32)

    dma = pltpu.SemaphoreType.DMA
    outs = (
        jax.ShapeDtypeStruct((2, 3, LEV, CE, CN), F32),
        jax.ShapeDtypeStruct((3, LEV, CE, CN), F32),
        jax.ShapeDtypeStruct((3, LEV, CE, CN), F32),
    )
    def array(*shape):
        return jax.ShapeDtypeStruct(shape, F32)

    held = (
        *outs[:2],
        *[array(5, SLABS, PITCH, CN)] * 3,
        *[array(3, SLABS, PITCH, CN)] * 3,
        array(15, LEV, CE, CN), array(3, LEV, CE, CN), array(LEV, CE, CN),
    )
    args = (
        disp_now, disp_prev, density, moduli, coarse, block_route, ranges,
        offsets.transpose(0, 3, 1, 2),
    )
    results = pl.pallas_call(
        kernel,
        out_shape=held,
        in_specs=[hbm] * 8,
        out_specs=(on_chip,) * len(held),
        scratch_shapes=[
            pltpu.SMEM((256,), jnp.int32), pltpu.SMEM((1, 1, 2), jnp.int32),
            pltpu.SMEM((1, 3, 1, 4), jnp.int32),
            vmem(3, LEV, CE, CN), vmem(2, 24, 256), vmem(24, 256),
            vmem(192, 128), pltpu.SMEM((4, NY * 4), jnp.int32),
            vmem(2, 3, 8, 128), vmem(NX * 3, 8, 128), vmem(NX * 3, 8, 128),
            vmem(2, NY, 48, 128), vmem(2, NY, 48, 128),
            pltpu.VMEM((64, 32), jnp.bfloat16), pltpu.VMEM((64, 16), jnp.bfloat16),
            pltpu.VMEM((4, 128, 256), jnp.bfloat16), pltpu.VMEM((4, 128, 256), jnp.bfloat16),
            *[vmem(12, SLABS, PITCH, CN)] * 3,
            vmem(4, 2, 48, 128), vmem(4, 2, 16, 128),
            vmem(4, 6, 48, 128), vmem(4, 2, 16, 128), vmem(6, 2, 8, 128),
            dma((4,)), dma((4,)), dma((2,)), dma((2,)), dma((2,)), dma((2,)),
            dma((8,)),
        ],
        compiler_params=pltpu.CompilerParams(
            collective_id=0, has_side_effects=True, vmem_limit_bytes=40 * 1024 * 1024
        ),
    )(*[pltpu.with_memory_space_constraint(v, pltpu.HBM) for v in args])
    return pl.pallas_call(
        finish,
        out_shape=outs,
        in_specs=[on_chip] * len(held),
        out_specs=(hbm, hbm, hbm),
        scratch_shapes=[vmem(3, LEV, CE, CN), dma((2 + PARTS,))],
        compiler_params=pltpu.CompilerParams(vmem_limit_bytes=4 * 1024 * 1024),
    )(*results)


def solution(mesh):
    return jax.shard_map(
        local,
        mesh=mesh,
        in_specs=(
            P(None, None, "gx", "gy"),
            P(None, None, "gx", "gy"),
            P(None, "gx", "gy"),
            P(None, None, "gx", "gy"),
            P(("gx", "gy"), None, None),
            P(),
            P("gx", "gy", None),
            P("gx", "gy", None, None),
        ),
        out_specs=(
            P(None, None, None, "gx", "gy"),
            P(None, None, "gx", "gy"),
            P(None, None, "gx", "gy"),
        ),
        check_vma=False,
    )
```
